512 devices in a mesh: dp: 32 (over y_hi, z), expert: 16 (over y_lo, x, core).
Axes of the slice: x: 4, y: 4 (y_hi: 2, y_lo: 2; y = y_hi * 2 + y_lo), z: 16, core: 2. Of those that a mesh axis runs over, the one named last changes fastest.
Arguments:
- residual_in: bfloat16 [1536, 2048], P('dp', 'expert'), may hold values from -36 to 36
- attention_values: bfloat16 [1536, 2048], P('dp', 'expert'), may hold values from -6 to 6
- out_weight: bfloat16 [2048, 2048], P('expert', 'dp'), may hold values from -0.25 to 0.25
- norm_gain: float32 [2048], replicated, may hold values from 0.1 to 1.9
- shared_gate: bfloat16 [2816, 2048], P('expert'), may hold values from -0.125 to 0.125
- shared_up: bfloat16 [2816, 2048], P('expert'), may hold values from -0.125 to 0.125
- shared_down: bfloat16 [2816, 2048], P('expert'), may hold values from -0.15625 to 0.15625
- expert_gate: bfloat16 [64, 1408, 2048], P('dp', 'expert'), may hold values from -0.125 to 0.125
- expert_up: bfloat16 [64, 1408, 2048], P('dp', 'expert'), may hold values from -0.125 to 0.125
- expert_down: bfloat16 [64, 1408, 2048], P('dp', 'expert'), may hold values from -0.21875 to 0.21875
- expert_ids: int32 [1536, 6], P('dp'), may hold values from 0 to 63, all different within a row; in each aligned block of 48 rows (0 to 47, 48 to 95, ...) at most 10 rows name the same one
- gate_weights: float32 [1536, 6], P('dp'), may hold values from 0.02 to 0.5
Outputs:
- layer_out: bfloat16 [1536, 2048], P('dp', 'expert')
The draws below stay inside these ranges and needn't reach their ends.
Inputs may be any that keep to these rules, and one draw needn't show every extreme that they name: `expert_ids`: each token names 6 different experts; among the 48 tokens of one index of dp (aligned blocks of rows) no expert is named by more than 10 tokens, a bound that some block reaches.
All inputs are finite; a program needn't handle non-finite values.
Results may differ from the reference program's by a relative error of at most 0.0035.
Values may be sent and summed in bfloat16 or wider, within the bound.
A program may use at most 128 MiB of HBM per device.

```python
import math
import jax
import jax.numpy as jnp
import numpy as np
from jax import lax

D = 2048
HEADS = 16
HEAD_V = 128
FFE = 1408
SHARED_FF = 2816
TOPK = 6
ROW_TOK = 48
EXPERTS = 64
TOKENS = 1536
CAP = 10
N_DP = 32


def draw_residual_in(key, part):
    first_key, second_key, third_key = jax.random.split(key, 3)
    base = jnp.clip(jax.random.normal(first_key, (TOKENS, D), jnp.float32), -4.0, 4.0)
    column_scale = jnp.exp(jax.random.uniform(second_key, (1, D), jnp.float32, math.log(0.3), math.log(3.0)))
    row_scale = jnp.exp(jax.random.uniform(third_key, (TOKENS, 1), jnp.float32, math.log(0.3), math.log(3.0)))
    return (base * column_scale * row_scale).astype(jnp.bfloat16)


def with_spikes(values, rng, source, target, parts, factor):
    def block_of(position):
        return (jnp.arange(values.shape[position]) // (values.shape[position] // parts)).reshape((-1,) + (1,) * (values.ndim - 1 - position))

    near = jax.random.permutation(rng, parts)[block_of(target)]
    second = (block_of(target) + parts // 2) % parts
    return jnp.where((block_of(source) == near) | (block_of(source) == second), factor * values, values)


def block_levels(stream_key, dims, pieces, least, top_value):
    level = 1.0
    for position, blocks in pieces:
        heights = jax.random.uniform(jax.random.fold_in(jax.random.fold_in(stream_key, 6), position), (blocks,), jnp.float32, least / len(pieces), top_value / len(pieces))
        level = level * jnp.repeat(jnp.exp(heights), dims[position] // blocks).reshape((-1,) + (1,) * (len(dims) - 1 - position))
    return level


def assign_block(key, own, number, rows, count, top, most, slope):
    sequence = jax.random.permutation(key, count)
    heavy_load, usual = load_shares(count, rows * top, most, slope, True), load_shares(count, rows * top, most, slope, False)
    places = jnp.arange(count)

    def named(tallies, rotation):
        used = int((tallies > 0).sum())
        fixed = max(1, used // 4)
        shifted = fixed + (places - fixed + rotation * (used - fixed)) % max(1, count - fixed)
        return jnp.zeros((count,), jnp.int32).at[sequence[jnp.where(places < fixed, places, shifted)]].set(jnp.asarray(tallies, jnp.int32))

    tallies = jnp.where(number % 4 == 0, named(heavy_load, number // 4), named(usual, number - number // 4 - 1))
    mixed = jax.random.permutation(jax.random.fold_in(own, 3), count)
    donor, taker = mixed[0:count // 2 * 2:2], mixed[1:count // 2 * 2:2]
    margin = jnp.minimum(tallies[donor] - 1, most - tallies[taker]) // 2
    margin = jnp.where((donor == sequence[0]) | (taker == sequence[0]) | (tallies[taker] == 0), 0, jnp.maximum(margin, 0))
    shifted = jax.random.randint(jax.random.fold_in(own, 4), (count // 2,), 0, 1 << 20) % (margin + 1)
    tallies = tallies.at[donor].add(-shifted).at[taker].add(shifted)
    items = jnp.searchsorted(jnp.cumsum(tallies), jnp.arange(rows * top), side="right").astype(jnp.int32)
    listing = items.reshape(top, rows).T
    listing = listing[jax.random.permutation(jax.random.fold_in(own, 1), rows)]
    rotation = jax.random.randint(jax.random.fold_in(own, 2), (rows, 1), 0, top)
    return jnp.take_along_axis(listing, (jnp.arange(top)[None, :] + rotation) % top, axis=1)


def load_shares(number_of, total, bound, lean, full):
    portions = [(1 << 20) // math.isqrt(rank ** lean) + 1 for rank in range(1, number_of + 1)]
    largest = bound if full else min(bound, max(-(-total // number_of), total * portions[0] // sum(portions)))
    least = 1 if total - largest >= number_of - 1 else 0
    holding, rest = [largest] + [least] * (number_of - 1), total - largest - least * (number_of - 1)
    while rest > 0:
        candidates = [i for i in range(1, number_of) if holding[i] < largest] or [i for i in range(1, number_of) if holding[i] < bound]
        mass, left = sum([portions[i] for i in candidates]), rest
        for i in candidates:
            more = min(bound - holding[i], max(1, left * portions[i] // mass), rest)
            holding[i] = holding[i] + more
            rest = rest - more
    return np.array(holding)


def normal_values(key, shape, deviation, limit, pieces=(), held_as=jnp.bfloat16):
    loudness = block_levels(key, shape, pieces, -0.22, 0.18) if pieces else 1.0
    array = jax.random.normal(key, shape, jnp.float32) * deviation * loudness
    return jnp.minimum(jnp.maximum(array, -limit), limit).astype(held_as)


def heavy_noise(key, shape, deviation, reach, pieces, heavy, kind=jnp.bfloat16):
    array = deviation * jax.random.normal(key, shape, jnp.float32)
    if pieces:
        array = array * block_levels(key, shape, pieces, -0.22, 0.18)
    return jnp.clip(with_spikes(array, jax.random.fold_in(key, 3), *heavy), -reach, reach).astype(kind)


def setup_inputs(seed: int = 0) -> dict:
    seeds = jax.random.split(jax.random.key(seed), 13)
    residual_in = draw_residual_in(jax.random.fold_in(seeds[12], 71), 0)
    attention_values = normal_values(seeds[1], (TOKENS, HEADS * HEAD_V), 1.0, 6.0, ((0, 32), (1, 16)))
    out_weight = heavy_noise(seeds[2], (HEADS * HEAD_V, D), (HEADS * HEAD_V) ** -0.5, 0.25, ((0, 16), (1, 32)), (0, 1, 32, 2.75))
    norm_gain = jnp.clip(1.0 + 0.18 * jax.random.normal(seeds[3], (D,), jnp.float32), 0.1, 1.9)
    shared_gate = normal_values(seeds[4], (SHARED_FF, D), D ** -0.5, 0.125, ((0, 16),))
    shared_up = normal_values(seeds[5], (SHARED_FF, D), D ** -0.5, 0.125, ((0, 16),))
    shared_down = heavy_noise(seeds[6], (SHARED_FF, D), SHARED_FF ** -0.5, 0.15625, ((0, 16),), (0, 1, 16, 2.0))
    expert_gate = normal_values(seeds[7], (EXPERTS, FFE, D), D ** -0.5, 0.125, ((0, 32), (1, 16)))
    expert_up = normal_values(seeds[8], (EXPERTS, FFE, D), D ** -0.5, 0.125, ((0, 32), (1, 16)))
    expert_down = heavy_noise(seeds[9], (EXPERTS, FFE, D), FFE ** -0.5, 0.21875, ((0, 32), (1, 16)), (1, 2, 16, 2.0))
    expert_ids_keys = jax.random.split(jax.random.fold_in(seeds[10], 1), TOKENS // ROW_TOK)
    expert_ids_turns = jax.random.permutation(jax.random.fold_in(seeds[10], 3), TOKENS // ROW_TOK)
    expert_ids = jax.vmap(lambda own, number: assign_block(jax.random.fold_in(seeds[10], 2), own, number, ROW_TOK, EXPERTS, TOPK, CAP, 1))(expert_ids_keys, expert_ids_turns).reshape((TOKENS, TOPK))
    gate_weights = jnp.clip(jnp.exp(math.log(0.5) - 3.218876 * jax.random.uniform(seeds[11], (TOKENS, TOPK), jnp.float32) ** block_levels(seeds[11], (TOKENS, TOPK), ((0, 32),), -0.2, 0.2)), 0.02, 0.5)
    return {"residual_in": residual_in, "attention_values": attention_values, "out_weight": out_weight, "norm_gain": norm_gain, "shared_gate": shared_gate, "shared_up": shared_up, "shared_down": shared_down, "expert_gate": expert_gate, "expert_up": expert_up, "expert_down": expert_down, "expert_ids": expert_ids, "gate_weights": gate_weights}


epsilon = 1e-06

def by_rows(left, right):
    return lax.dot_general(left, right, (((1,), (1,)), ((), ())), preferred_element_type=jnp.float32)

def reference(residual_in, attention_values, out_weight, norm_gain, shared_gate, shared_up, shared_down, expert_gate, expert_up, expert_down, expert_ids, gate_weights):
    residual = residual_in.astype(jnp.float32) + jnp.dot(attention_values, out_weight, preferred_element_type=jnp.float32)
    inverse_rms = lax.rsqrt(lax.optimization_barrier(jnp.mean(residual * residual, axis=1, keepdims=True)) + epsilon)
    normed = (residual * inverse_rms * norm_gain).astype(jnp.bfloat16)
    shared_active = (jax.nn.silu(by_rows(normed, shared_gate)) * by_rows(normed, shared_up)).astype(jnp.bfloat16)
    shared_terms = jnp.dot(shared_active, shared_down, preferred_element_type=jnp.float32)
    slot_count = N_DP * CAP

    def one_expert(routed, inputs):
        number, gate_matrix, up_matrix, down_matrix = inputs
        matched = expert_ids == number
        chosen = jnp.any(matched, axis=1)
        weights = lax.optimization_barrier(jnp.sum(jnp.where(matched, gate_weights, 0.0), axis=1))
        picked_rows = jnp.nonzero(chosen, size=slot_count, fill_value=0)[0].astype(jnp.int32)
        in_use = jnp.arange(slot_count, dtype=jnp.int32) < jnp.sum(chosen.astype(jnp.int32))
        picked = normed[picked_rows]
        active = (jax.nn.silu(by_rows(picked, gate_matrix)) * by_rows(picked, up_matrix)).astype(jnp.bfloat16)
        factor = jnp.where(in_use, weights[picked_rows], 0.0)
        contrib = jnp.dot(active, down_matrix, preferred_element_type=jnp.float32) * factor[:, None]
        return (routed.at[picked_rows].add(contrib), None)
    routed, _ = lax.scan(one_expert, jnp.zeros((TOKENS, D), jnp.float32), (jnp.arange(EXPERTS, dtype=jnp.int32), expert_gate, expert_up, expert_down))
    return (residual + shared_terms + routed).astype(jnp.bfloat16)
```

```python
import jax
import jax.numpy as jnp
from jax import lax
from jax.experimental import pallas as pl
from jax.experimental.pallas import tpu as pltpu
from jax.sharding import PartitionSpec as P

MESH = pl.DeviceIdType.MESH
epsilon = 1e-06
DP = 32
EX = 16
CAP = 10
RB = 32
LANE = 128
F32 = jnp.float32
BF16 = jnp.bfloat16


def by_rows(left, right):
    return lax.dot_general(left, right, (((1,), (1,)), ((), ())), preferred_element_type=F32)


def by_columns(left, right):
    return lax.dot_general(left, right, (((0,), (0,)), ((), ())), preferred_element_type=F32)


def iota(shape, dim):
    return lax.broadcasted_iota(jnp.int32, shape, dim)


def silu(v):
    return v / (1.0 + jnp.exp(-v))


def loop(start, stop, body):
    def step(j, carry):
        body(j)
        return carry

    lax.fori_loop(start, stop, step, 0)


def layer_kernel(
    res_in, attn, w_in, gain, sh_gate, sh_up, sh_down, ex_gate, ex_up, ex_down, ids, weights,
    out,
    wt, w_all, part, rs_buf, res_all, normed, xs, xr, x_all, a_all, d_all, s_part, s_buf, ys, yr,
    pack, unpack, sel, comb,
    w_send, w_recv, d_send, d_recv, r_send, r_recv, g_send, g_recv, x_send, x_recv,
    xa_send, xa_recv, s_send, s_recv, aa_send, aa_recv, y_send, y_recv, own_sem,
):
    d = lax.axis_index("dp")
    e = lax.axis_index("expert")
    rows = res_in.shape[0]
    hidden = ex_gate.shape[1]
    locals_ = ex_gate.shape[0]
    per_expert = DP * CAP

    def rcopy(src, dst, send, recv, device):
        return pltpu.make_async_remote_copy(
            src_ref=src, dst_ref=dst, send_sem=send, recv_sem=recv,
            device_id=device, device_id_type=MESH,
        )

    barrier = pltpu.get_barrier_semaphore()

    def greet_dp(j):
        pl.semaphore_signal(barrier, inc=1, device_id=((d + j) % DP, e), device_id_type=MESH)

    def greet_expert(j):
        pl.semaphore_signal(barrier, inc=1, device_id=(d, (e + j) % EX), device_id_type=MESH)

    loop(1, DP, greet_dp)
    loop(1, EX, greet_expert)

    wt[...] = w_in[...].astype(F32).T.astype(BF16)
    w_all[d] = wt[...]
    own_down = pltpu.make_async_copy(
        ex_down.at[:, :, pl.ds(pl.multiple_of(e * LANE, LANE), LANE)], d_all.at[e], own_sem
    )
    own_down.start()
    named = jnp.zeros((rows, 64), F32)
    experts_iota = iota((rows, 64), 1)
    for k in range(ids.shape[1]):
        named = named + (ids[:, k : k + 1] == experts_iota).astype(F32)
    lower = (iota((rows, rows), 1) < iota((rows, rows), 0)).astype(F32)
    earlier = jnp.dot(lower, named, preferred_element_type=F32)
    slots_iota = iota((rows, DP * RB), 1).astype(F32)
    sel_sum = jnp.zeros((rows, DP * RB), F32)
    comb_sum = jnp.zeros((rows, DP * RB), F32)
    for k in range(ids.shape[1]):
        own = ids[:, k : k + 1]
        place = jnp.sum(jnp.where(own == experts_iota, earlier, 0.0), axis=1, keepdims=True)
        slot = ((own >> 1) * RB + (own & 1) * CAP).astype(F32) + place
        hit = slots_iota == slot
        sel_sum = sel_sum + jnp.where(hit, 1.0, 0.0)
        comb_sum = comb_sum + jnp.where(hit, weights[:, k : k + 1], 0.0)
    sel[...] = sel_sum.astype(BF16)
    comb[...] = comb_sum

    def packed_row(j):
        inner = j & (RB - 1)
        second = (inner >= CAP).astype(jnp.int32)
        row = second * (per_expert - CAP) + (j >> 5) * CAP + inner
        return jnp.where(inner < 2 * CAP, row, -1)

    total = locals_ * per_expert
    pack[...] = (
        packed_row(iota((1, DP * RB), 1)) == iota((total, DP * RB), 0)
    ).astype(F32).astype(BF16)
    unpack[...] = (
        packed_row(iota((DP * RB, 1), 0)) == iota((DP * RB, total), 1)
    ).astype(F32).astype(BF16)

    pl.semaphore_wait(barrier, DP - 1 + EX - 1)

    group = (d // 16) * 4 + (d % 16) // 4
    place4 = d % 4
    run_base = d - place4

    def member(q):
        return (q // 4) * 16 + (q % 4) * 4 + place4

    def send_far(j):
        rcopy(
            wt, w_all.at[d], w_send.at[j], w_recv.at[d], (member((group + j) % 8), e)
        ).start()

    def send_near(src_ref, src, number):
        for i in range(1, 4):
            rcopy(
                src_ref, w_all.at[src], w_send.at[8 + number * 3 + i - 1], w_recv.at[src],
                (run_base + (place4 + i) % 4, e),
            ).start()

    loop(1, 8, send_far)
    send_near(wt, d, 0)

    def down_copy(j):
        other = (e + j) % EX
        return rcopy(
            ex_down.at[:, :, pl.ds(pl.multiple_of(other * LANE, LANE), LANE)], d_all.at[e],
            d_send.at[j], d_recv.at[e], (d, other),
        )

    loop(1, EX, lambda j: down_copy(j).start())

    def relay(j):
        src = member((group - j + 8) % 8)
        rcopy(w_all.at[src], w_all.at[src], w_send.at[0], w_recv.at[src], (src, e)).wait_recv()
        send_near(w_all.at[src], src, j)

    loop(1, 8, relay)

    def near_arrival(j):
        other = run_base + (place4 + 1 + j // 8) % 4
        src = ((j % 8) // 4) * 16 + (j % 4) * 4 + other % 4
        rcopy(w_all.at[src], w_all.at[src], w_send.at[0], w_recv.at[src], (other, e)).wait_recv()

    loop(0, 24, near_arrival)

    head = by_rows(attn[...], w_all[...].reshape(DP * w_all.shape[1], LANE))
    for i in range(EX):
        part[i] = head[:, i * LANE : (i + 1) * LANE]

    def direct(src_of, dst, send, recv, j):
        other = (e + j) % EX
        return rcopy(src_of(other), dst.at[e], send.at[j], recv.at[e], (d, other))

    def direct_arrival(dst, send, recv, j):
        src = (e + EX - j) % EX
        rcopy(dst.at[src], dst.at[src], send.at[0], recv.at[src], (d, src)).wait_recv()

    loop(1, EX, lambda j: direct(lambda o: part.at[o], rs_buf, r_send, r_recv, j).start())
    rs_buf[e] = part[e]
    loop(1, EX, lambda j: direct_arrival(rs_buf, r_send, r_recv, j))
    residual = res_in[...].astype(F32) + jnp.sum(rs_buf[...], axis=0)
    res_all[e] = residual
    loop(1, EX, lambda j: direct(lambda o: res_all.at[e], res_all, g_send, g_recv, j).start())
    loop(1, EX, lambda j: direct_arrival(res_all, g_send, g_recv, j))

    squares = jnp.zeros((rows, LANE), F32)
    for i in range(EX):
        squares = squares + res_all[i] * res_all[i]
    mean = jnp.sum(squares, axis=1, keepdims=True) / (EX * LANE)
    inverse_rms = lax.rsqrt(mean + epsilon)

    normed_own = (residual * inverse_rms * gain[pl.ds(e, 1), :]).astype(BF16)
    xs[...] = by_columns(sel[...], normed_own).astype(BF16).reshape(DP, RB, LANE)

    def over_dp(src, dst, send, recv, j):
        other = (d + j) % DP
        return rcopy(src.at[other], dst.at[d], send.at[j], recv.at[d], (other, e))

    def dp_arrival(dst, send, recv, j):
        src = (d + DP - j) % DP
        rcopy(dst.at[src], dst.at[src], send.at[0], recv.at[src], (src, e)).wait_recv()

    loop(1, DP, lambda j: over_dp(xs, xr, x_send, x_recv, j).start())
    xr[d] = xs[d]

    for i in range(EX):
        normed[:, i * LANE : (i + 1) * LANE] = (
            res_all[i] * inverse_rms * gain[i : i + 1, :]
        ).astype(BF16)
    normed_rows = normed[...]
    shared_active = (
        silu(by_rows(normed_rows, sh_gate[...])) * by_rows(normed_rows, sh_up[...])
    ).astype(BF16)
    shared = jnp.dot(shared_active, sh_down[...], preferred_element_type=F32)
    for i in range(EX):
        s_part[i] = shared[:, i * LANE : (i + 1) * LANE]
    loop(1, EX, lambda j: direct(lambda o: s_part.at[o], s_buf, s_send, s_recv, j).start())
    s_buf[e] = s_part[e]

    loop(1, DP, lambda j: dp_arrival(xr, x_send, x_recv, j))

    chip = e // 2
    core = e % 2
    sibling = e + 1 - 2 * core

    def gather(buf, send, recv):
        def to_chip(j):
            other = ((chip + j) % 8) * 2 + core
            rcopy(buf.at[e], buf.at[e], send.at[j], recv.at[e], (d, other)).start()

        def onward(src, j):
            rcopy(buf.at[src], buf.at[src], send.at[8 + j], recv.at[src], (d, sibling)).start()

        def arrive(j):
            src = ((chip - j + 8) % 8) * 2 + core
            rcopy(buf.at[src], buf.at[src], send.at[0], recv.at[src], (d, src)).wait_recv()
            onward(src, j)

        def from_sibling(j):
            src = ((chip - j + 8) % 8) * 2 + 1 - core
            rcopy(buf.at[src], buf.at[src], send.at[0], recv.at[src], (d, sibling)).wait_recv()

        loop(1, 8, to_chip)
        onward(e, 0)
        loop(1, 8, arrive)
        loop(0, 8, from_sibling)

    def gather_sent(buf, send, recv):
        def sent(j):
            rcopy(buf.at[e], buf.at[e], send.at[j], recv.at[e], (d, sibling)).wait_send()

        loop(1, 16, sent)

    x_all[e] = jnp.dot(
        pack[...], xr[...].reshape(DP * RB, LANE), preferred_element_type=F32
    ).astype(BF16)
    gather(x_all, xa_send, xa_recv)

    for l in range(locals_):
        span = slice(l * per_expert, (l + 1) * per_expert)
        tokens = jnp.concatenate([x_all[i, span, :] for i in range(EX)], axis=1)
        a_all[e, span, :] = (
            silu(by_rows(tokens, ex_gate[l])) * by_rows(tokens, ex_up[l])
        ).astype(BF16)
    gather(a_all, aa_send, aa_recv)

    own_down.wait()
    loop(1, EX, lambda j: direct_arrival(d_all, d_send, d_recv, j))
    results = []
    for l in range(locals_):
        span = slice(l * per_expert, (l + 1) * per_expert)
        y = jnp.zeros((per_expert, LANE), F32)
        for i in range(EX):
            y = y + jnp.dot(a_all[i, span, :], d_all[i, l], preferred_element_type=F32)
        results.append(y.astype(BF16))
    y_rows = jnp.concatenate(results, axis=0)
    ys[...] = (
        jnp.dot(unpack[...], y_rows, preferred_element_type=F32)
        .astype(BF16)
        .reshape(DP, RB, LANE)
    )
    loop(1, DP, lambda j: over_dp(ys, yr, y_send, y_recv, j).start())
    yr[d] = ys[d]

    loop(1, EX, lambda j: direct_arrival(s_buf, s_send, s_recv, j))
    base = res_all[e] + jnp.sum(s_buf[...], axis=0)
    loop(1, DP, lambda j: dp_arrival(yr, y_send, y_recv, j))
    routed = lax.dot_general(
        comb[...], yr[...].reshape(DP * RB, LANE).astype(F32), (((1,), (0,)), ((), ())),
        precision=lax.Precision.HIGHEST, preferred_element_type=F32,
    )
    out[...] = (base + routed).astype(BF16)

    loop(
        1, 32,
        lambda j: rcopy(wt, w_all.at[d], w_send.at[j], w_recv.at[d], (d, sibling)).wait_send(),
    )
    loop(1, EX, lambda j: down_copy(j).wait_send())
    loop(1, EX, lambda j: direct(lambda o: part.at[o], rs_buf, r_send, r_recv, j).wait_send())
    loop(1, EX, lambda j: direct(lambda o: res_all.at[e], res_all, g_send, g_recv, j).wait_send())
    loop(1, EX, lambda j: direct(lambda o: s_part.at[o], s_buf, s_send, s_recv, j).wait_send())
    loop(1, DP, lambda j: over_dp(xs, xr, x_send, x_recv, j).wait_send())
    loop(1, DP, lambda j: over_dp(ys, yr, y_send, y_recv, j).wait_send())
    gather_sent(x_all, xa_send, xa_recv)
    gather_sent(a_all, aa_send, aa_recv)


def shards(
    residual_in, attention_values, out_weight, norm_gain, shared_gate, shared_up, shared_down,
    expert_gate, expert_up, expert_down, expert_ids, gate_weights,
):
    rows = residual_in.shape[0]
    local, hidden, width = expert_gate.shape
    total = local * DP * CAP
    vmem = pl.BlockSpec(memory_space=pltpu.VMEM)

    def sems(n):
        return [pltpu.SemaphoreType.DMA((n,))] * 2

    return pl.pallas_call(
        layer_kernel,
        out_shape=jax.ShapeDtypeStruct((rows, LANE), BF16),
        in_specs=[vmem] * 12,
        out_specs=vmem,
        scratch_shapes=[
            pltpu.VMEM((width // DP, LANE), BF16),
            pltpu.VMEM((DP, width // DP, LANE), BF16),
            pltpu.VMEM((EX, rows, LANE), F32),
            pltpu.VMEM((EX, rows, LANE), F32),
            pltpu.VMEM((EX, rows, LANE), F32),
            pltpu.VMEM((rows, width), BF16),
            pltpu.VMEM((DP, RB, LANE), BF16),
            pltpu.VMEM((DP, RB, LANE), BF16),
            pltpu.VMEM((EX, total, LANE), BF16),
            pltpu.VMEM((EX, total, hidden), BF16),
            pltpu.VMEM((EX, local, hidden, LANE), BF16),
            pltpu.VMEM((EX, rows, LANE), F32),
            pltpu.VMEM((EX, rows, LANE), F32),
            pltpu.VMEM((DP, RB, LANE), BF16),
            pltpu.VMEM((DP, RB, LANE), BF16),
            pltpu.VMEM((total, DP * RB), BF16),
            pltpu.VMEM((DP * RB, total), BF16),
            pltpu.VMEM((rows, DP * RB), BF16),
            pltpu.VMEM((rows, DP * RB), F32),
        ]
        + sems(32) + sems(EX) + sems(EX) + sems(EX) + sems(DP)
        + sems(EX) + sems(EX) + sems(EX) + sems(DP)
        + [pltpu.SemaphoreType.DMA(())],
        compiler_params=pltpu.CompilerParams(
            collective_id=0, has_side_effects=True, vmem_limit_bytes=60 * 1024 * 1024
        ),
        name="layer",
    )(
        residual_in, attention_values, out_weight, norm_gain.reshape(EX, LANE),
        shared_gate, shared_up, shared_down, expert_gate, expert_up, expert_down,
        expert_ids, gate_weights,
    )


def solution(mesh):
    return jax.shard_map(
        shards,
        mesh=mesh,
        in_specs=(
            P("dp", "expert"),
            P("dp", "expert"),
            P("expert", "dp"),
            P(),
            P("expert", None),
            P("expert", None),
            P("expert", None),
            P("dp", "expert", None),
            P("dp", "expert", None),
            P("dp", "expert", None),
            P("dp", None),
            P("dp", None),
        ),
        out_specs=P("dp", "expert"),
        check_vma=False,
    )
```

```python
import jax
import jax.numpy as jnp
from jax import lax
from jax.experimental import pallas as pl
from jax.experimental.pallas import tpu as pltpu
from jax.sharding import PartitionSpec as P

MESH = pl.DeviceIdType.MESH
epsilon = 1e-06
DP = 32
EX = 16
CAP = 10
RB = 16
LANE = 128
F32 = jnp.float32
BF16 = jnp.bfloat16


def by_rows(left, right):
    return lax.dot_general(left, right, (((1,), (1,)), ((), ())), preferred_element_type=F32)


def by_columns(left, right):
    return lax.dot_general(left, right, (((0,), (0,)), ((), ())), preferred_element_type=F32)


def iota(shape, dim):
    return lax.broadcasted_iota(jnp.int32, shape, dim)


def silu(v):
    return v / (1.0 + jnp.exp(-v))


def loop(start, stop, body):
    def step(j, carry):
        body(j)
        return carry

    lax.fori_loop(start, stop, step, 0)


def layer_kernel(
    res_in, attn, w_in, gain, sh_gate_in, sh_up_in, sh_down_in, ex_gate_in, ex_up_in, ex_down,
    ids, weights,
    out,
    sh_gate, sh_up, sh_down, ex_gate, ex_up,
    w_all, part, rs_buf, res_all, xs, xr, x_all, a_all, d_all, s_part, s_buf, ys, yr,
    pack, unpack, sel, comb,
    in_sem, w_send, w_recv, d_send, d_recv, r_send, r_recv, g_send, g_recv, x_send, x_recv,
    xa_send, xa_recv, s_send, s_recv, aa_send, aa_recv, y_send, y_recv,
):
    d = lax.axis_index("dp")
    e = lax.axis_index("expert")
    rows = res_in.shape[0]
    local = ex_gate.shape[0]
    per_expert = DP * CAP
    slots = DP * RB

    def rcopy(src, dst, send, recv, device):
        return pltpu.make_async_remote_copy(
            src_ref=src, dst_ref=dst, send_sem=send, recv_sem=recv,
            device_id=device, device_id_type=MESH,
        )

    def arrival(ref, recv, send, device):
        rcopy(ref, ref, send, recv, device).wait_recv()

    barrier = pltpu.get_barrier_semaphore()

    def greet_dp(j):
        pl.semaphore_signal(barrier, inc=1, device_id=((d + j) % DP, e), device_id_type=MESH)

    def greet_expert(j):
        pl.semaphore_signal(barrier, inc=1, device_id=(d, (e + j) % EX), device_id_type=MESH)

    loop(1, DP, greet_dp)
    loop(1, EX, greet_expert)

    def own_columns(other):
        return ex_down.at[:, :, pl.ds(pl.multiple_of(other * LANE, LANE), LANE)]

    loads = [
        pltpu.make_async_copy(src, dst, in_sem.at[n])
        for n, (src, dst) in enumerate(
            [
                (sh_gate_in, sh_gate), (sh_up_in, sh_up), (sh_down_in, sh_down),
                (ex_gate_in, ex_gate), (ex_up_in, ex_up), (own_columns(e), d_all.at[e]),
            ]
        )
    ]
    for copy in loads:
        copy.start()
    w_all[d] = w_in[...]
    experts_iota = iota((64, rows), 0)
    named = jnp.zeros((64, rows), F32)
    for k in range(ids.shape[0]):
        named = named + (ids[k : k + 1, :] == experts_iota).astype(F32)
    upper = (iota((rows, rows), 0) < iota((rows, rows), 1)).astype(F32)
    earlier = jnp.dot(named, upper, preferred_element_type=F32)
    slots_iota = iota((local * slots, rows), 0).astype(F32)
    sel_sum = jnp.zeros((local * slots, rows), F32)
    comb_sum = jnp.zeros((local * slots, rows), F32)
    for k in range(ids.shape[0]):
        own = ids[k : k + 1, :]
        place = jnp.sum(jnp.where(own == experts_iota, earlier, 0.0), axis=0, keepdims=True)
        slot = ((own & 1) * slots + (own >> 1) * RB).astype(F32) + place
        hit = slots_iota == slot
        sel_sum = sel_sum + jnp.where(hit, 1.0, 0.0)
        comb_sum = comb_sum + jnp.where(hit, weights[k : k + 1, :], 0.0)
    sel[...] = sel_sum.astype(BF16)
    comb[...] = comb_sum

    def packed_row(j):
        inner = j & (RB - 1)
        return jnp.where(inner < CAP, (j >> 4) * CAP + inner, -1)

    pack[...] = (
        packed_row(iota((1, slots), 1)) == iota((per_expert, slots), 0)
    ).astype(F32).astype(BF16)
    unpack[...] = (
        packed_row(iota((slots, 1), 0)) == iota((slots, per_expert), 1)
    ).astype(F32).astype(BF16)

    pl.semaphore_wait(barrier, DP - 1 + EX - 1)

    z = d % 16
    row = d - z
    kind = z % 4
    group = (d // 16) * 4 + z // 4
    above = row + (z + 1) % 16
    below = row + (z + 15) % 16

    def member(q, of):
        return (q // 4) * 16 + (q % 4) * 4 + of

    def w_copy(src, n, device):
        return rcopy(w_all.at[src], w_all.at[src], w_send.at[n], w_recv.at[src], (device, e))

    loop(1, 8, lambda j: rcopy(
        w_in, w_all.at[d], w_send.at[j], w_recv.at[d], (member((group + j) % 8, kind), e)
    ).start())
    for n, device in ((8, above), (9, below)):
        rcopy(w_in, w_all.at[d], w_send.at[n], w_recv.at[d], (device, e)).start()

    def down_copy(j):
        other = (e + j) % EX
        return rcopy(own_columns(other), d_all.at[e], d_send.at[j], d_recv.at[e], (d, other))

    loop(1, EX, lambda j: down_copy(j).start())

    def w_arrival(src, device):
        arrival(w_all.at[src], w_recv.at[src], w_send.at[0], (device, e))

    def far_arrival(j):
        src = member((group + 8 - j) % 8, kind)
        w_arrival(src, src)
        w_copy(src, 8 + 2 * j, above).start()
        w_copy(src, 9 + 2 * j, below).start()

    loop(1, 8, far_arrival)

    def near_low(q):
        src = member(q, (kind + 3) % 4)
        w_arrival(src, below)
        w_copy(src, 24 + q, above).start()
        w_arrival(member(q, (kind + 1) % 4), above)

    def near_high(q):
        src = member(q, (kind + 1) % 4)
        w_arrival(src, above)
        w_copy(src, 24 + q, below).start()
        w_arrival(member(q, (kind + 3) % 4), below)

    loop(0, 4, near_low)
    loop(4, 8, near_high)
    loop(0, 4, lambda q: w_arrival(member(q, (kind + 2) % 4), below))
    loop(4, 8, lambda q: w_arrival(member(q, (kind + 2) % 4), above))

    head = by_rows(attn[...], w_all[...].reshape(DP * w_all.shape[1], LANE))
    for i in range(EX):
        part[i] = head[:, i * LANE : (i + 1) * LANE]

    def direct(src, dst, send, recv, j):
        other = (e + j) % EX
        return rcopy(src.at[other], dst.at[e], send.at[j], recv.at[e], (d, other))

    def direct_arrival(dst, send, recv, j):
        src = (e + EX - j) % EX
        arrival(dst.at[src], recv.at[src], send.at[0], (d, src))

    core = e % 2
    x = (e // 2) % 4
    y = e // 8

    def at(right, other_row):
        yy = y if other_row == 0 else 1 - y
        return (yy * 4 + (x + right) % 4) * 2 + core

    left, right, across = at(3, 0), at(1, 0), at(0, 1)
    sibling = e + 1 - 2 * core

    def gather_start(buf, l, send, recv):
        for n, device in ((1, right), (2, left), (3, across), (4, sibling)):
            rcopy(
                buf.at[l, e], buf.at[l, e], send.at[l, n], recv.at[l, e], (d, device)
            ).start()

    def gather_rest(buf, l, send, recv):
        def take(src, device):
            arrival(buf.at[l, src], recv.at[l, src], send.at[l, 0], (d, device))

        def on(src, n, device):
            rcopy(
                buf.at[l, src], buf.at[l, src], send.at[l, n], recv.at[l, src], (d, device)
            ).start()

        src = left
        take(src, left)
        on(src, 5, right * (1 - core) + across * core)
        on(src, 6, sibling)
        src = across
        take(src, across)

        @pl.when(core == 0)
        def _():
            on(across, 7, right)
            on(across, 8, left)

        on(src, 9, sibling)
        src = right
        take(src, right)

        @pl.when(core == 1)
        def _():
            on(right, 7, left)
            on(right, 8, across)

        on(src, 10, sibling)
        src = at(1, 1)
        take(src, right * (1 - core) + across * core)

        @pl.when(core == 0)
        def _():
            on(at(1, 1), 11, left)

        on(src, 12, sibling)
        src = at(2, 0)
        take(src, left * (1 - core) + right * core)

        @pl.when(core == 1)
        def _():
            on(at(2, 0), 11, across)

        on(src, 13, sibling)
        src = at(3, 1)
        take(src, left * (1 - core) + across * core)
        on(src, 14, sibling)
        src = at(2, 1)
        take(src, right * (1 - core) + across * core)
        on(src, 15, sibling)

        def from_sibling(chip):
            take(chip * 2 + 1 - core, sibling)

        loop(0, 8, from_sibling)

    def gather_sent(buf, l, send, recv):
        loop(
            1, 16,
            lambda n: rcopy(
                buf.at[l, e], buf.at[l, e], send.at[l, n], recv.at[l, e], (d, sibling)
            ).wait_send(),
        )

    loop(1, EX, lambda j: direct(part, rs_buf, r_send, r_recv, j).start())
    rs_buf[e] = part[e]
    loop(1, EX, lambda j: direct_arrival(rs_buf, r_send, r_recv, j))
    residual = res_in[...].astype(F32) + jnp.sum(rs_buf[...], axis=0)
    res_all[0, e] = residual
    gather_start(res_all, 0, g_send, g_recv)
    gather_rest(res_all, 0, g_send, g_recv)

    squares = jnp.zeros((rows, LANE), F32)
    for i in range(EX):
        squares = squares + res_all[0, i] * res_all[0, i]
    mean = jnp.sum(squares, axis=1, keepdims=True) / (EX * LANE)
    inverse_rms = lax.rsqrt(mean + epsilon)

    normed_own = (residual * inverse_rms * gain[pl.ds(e, 1), :]).astype(BF16)

    def over_dp(src, dst, l, send, recv, j):
        other = (d + j) % DP
        return rcopy(src.at[l, other], dst.at[l, d], send.at[l, j], recv.at[l, d], (other, e))

    def dp_arrival(dst, l, send, recv, j):
        src = (d + DP - j) % DP
        arrival(dst.at[l, src], recv.at[l, src], send.at[l, 0], (src, e))

    for l in range(local):
        xs[l] = (
            jnp.dot(
                sel[l * slots : (l + 1) * slots, :], normed_own, preferred_element_type=F32
            ).astype(BF16).reshape(DP, RB, LANE)
        )
        loop(1, DP, lambda j: over_dp(xs, xr, l, x_send, x_recv, j).start())
        xr[l, d] = xs[l, d]

    for copy in loads:
        copy.wait()
    normed = jnp.concatenate(
        [(res_all[0, i] * inverse_rms * gain[i : i + 1, :]).astype(BF16) for i in range(EX)],
        axis=1,
    )
    shared_active = (
        silu(by_rows(normed, sh_gate[...])) * by_rows(normed, sh_up[...])
    ).astype(BF16)
    shared = jnp.dot(shared_active, sh_down[...], preferred_element_type=F32)
    for i in range(EX):
        s_part[i] = shared[:, i * LANE : (i + 1) * LANE]
    s_buf[e] = s_part[e]

    def take_rows(l):
        loop(1, DP, lambda j: dp_arrival(xr, l, x_send, x_recv, j))
        x_all[l, e] = jnp.dot(
            pack[...], xr[l].reshape(slots, LANE), preferred_element_type=F32
        ).astype(BF16)
        gather_start(x_all, l, xa_send, xa_recv)

    def activate(l):
        tokens = jnp.concatenate([x_all[l, i] for i in range(EX)], axis=1)
        a_all[l, e] = (
            silu(by_rows(tokens, ex_gate[l])) * by_rows(tokens, ex_up[l])
        ).astype(BF16)
        gather_start(a_all, l, aa_send, aa_recv)

    def send_back(l):
        y_rows = jnp.zeros((per_expert, LANE), F32)
        for i in range(EX):
            y_rows = y_rows + jnp.dot(a_all[l, i], d_all[i, l], preferred_element_type=F32)
        ys[l] = (
            jnp.dot(unpack[...], y_rows.astype(BF16), preferred_element_type=F32)
            .astype(BF16)
            .reshape(DP, RB, LANE)
        )
        loop(1, DP, lambda j: over_dp(ys, yr, l, y_send, y_recv, j).start())
        yr[l, d] = ys[l, d]

    def collect(l):
        loop(1, DP, lambda j: dp_arrival(yr, l, y_send, y_recv, j))
        return lax.dot_general(
            comb[l * slots : (l + 1) * slots, :], yr[l].reshape(slots, LANE).astype(F32),
            (((0,), (0,)), ((), ())),
            precision=lax.Precision.HIGHEST, preferred_element_type=F32,
        )

    take_rows(0)
    gather_rest(x_all, 0, xa_send, xa_recv)
    take_rows(1)
    activate(0)
    gather_rest(x_all, 1, xa_send, xa_recv)
    activate(1)
    gather_rest(a_all, 0, aa_send, aa_recv)
    loop(1, EX, lambda j: direct_arrival(d_all, d_send, d_recv, j))
    send_back(0)
    gather_rest(a_all, 1, aa_send, aa_recv)
    send_back(1)
    loop(1, EX, lambda j: direct(s_part, s_buf, s_send, s_recv, j).start())
    routed = collect(0)
    loop(1, EX, lambda j: direct_arrival(s_buf, s_send, s_recv, j))
    base = residual + jnp.sum(s_buf[...], axis=0)
    routed = routed + collect(1)
    out[...] = (base + routed).astype(BF16)

    loop(1, 32, lambda n: w_copy(d, n, above).wait_send())
    loop(1, EX, lambda j: down_copy(j).wait_send())
    loop(1, EX, lambda j: direct(part, rs_buf, r_send, r_recv, j).wait_send())
    loop(1, EX, lambda j: direct(s_part, s_buf, s_send, s_recv, j).wait_send())
    gather_sent(res_all, 0, g_send, g_recv)
    for l in range(local):
        loop(1, DP, lambda j: over_dp(xs, xr, l, x_send, x_recv, j).wait_send())
        loop(1, DP, lambda j: over_dp(ys, yr, l, y_send, y_recv, j).wait_send())
        gather_sent(x_all, l, xa_send, xa_recv)
        gather_sent(a_all, l, aa_send, aa_recv)


def shards(
    residual_in, attention_values, out_weight, norm_gain, shared_gate, shared_up, shared_down,
    expert_gate, expert_up, expert_down, expert_ids, gate_weights,
):
    rows = residual_in.shape[0]
    local, hidden, width = expert_gate.shape
    per_expert = DP * CAP
    vmem = pl.BlockSpec(memory_space=pltpu.VMEM)
    hbm = pl.BlockSpec(memory_space=pl.ANY)

    def sems(*shape):
        return [pltpu.SemaphoreType.DMA(shape)] * 2

    def like(array):
        return pltpu.VMEM(array.shape, array.dtype)

    return pl.pallas_call(
        layer_kernel,
        out_shape=jax.ShapeDtypeStruct((rows, LANE), BF16),
        in_specs=[vmem] * 4 + [hbm] * 6 + [vmem] * 2,
        out_specs=vmem,
        scratch_shapes=[
            like(shared_gate), like(shared_up), like(shared_down), like(expert_gate),
            like(expert_up),
            pltpu.VMEM((DP, width // DP, LANE), BF16),
            pltpu.VMEM((EX, rows, LANE), F32),
            pltpu.VMEM((EX, rows, LANE), F32),
            pltpu.VMEM((1, EX, rows, LANE), F32),
            pltpu.VMEM((local, DP, RB, LANE), BF16),
            pltpu.VMEM((local, DP, RB, LANE), BF16),
            pltpu.VMEM((local, EX, per_expert, LANE), BF16),
            pltpu.VMEM((local, EX, per_expert, hidden), BF16),
            pltpu.VMEM((EX, local, hidden, LANE), BF16),
            pltpu.VMEM((EX, rows, LANE), F32),
            pltpu.VMEM((EX, rows, LANE), F32),
            pltpu.VMEM((local, DP, RB, LANE), BF16),
            pltpu.VMEM((local, DP, RB, LANE), BF16),
            pltpu.VMEM((per_expert, DP * RB), BF16),
            pltpu.VMEM((DP * RB, per_expert), BF16),
            pltpu.VMEM((local * DP * RB, rows), BF16),
            pltpu.VMEM((local * DP * RB, rows), F32),
            pltpu.SemaphoreType.DMA((6,)),
        ]
        + sems(DP) + sems(EX) + sems(EX) + sems(1, EX) + sems(local, DP)
        + sems(local, EX) + sems(EX) + sems(local, EX) + sems(local, DP),
        compiler_params=pltpu.CompilerParams(
            collective_id=0, has_side_effects=True, vmem_limit_bytes=60 * 1024 * 1024
        ),
        name="layer",
    )(
        residual_in, attention_values, out_weight.T, norm_gain.reshape(EX, LANE),
        shared_gate, shared_up, shared_down, expert_gate, expert_up, expert_down,
        expert_ids.T, gate_weights.T,
    )


def solution(mesh):
    return jax.shard_map(
        shards,
        mesh=mesh,
        in_specs=(
            P("dp", "expert"),
            P("dp", "expert"),
            P("expert", "dp"),
            P(),
            P("expert", None),
            P("expert", None),
            P("expert", None),
            P("dp", "expert", None),
            P("dp", "expert", None),
            P("dp", "expert", None),
            P("dp", None),
            P("dp", None),
        ),
        out_specs=P("dp", "expert"),
        check_vma=False,
    )
```

```python
import jax
import jax.numpy as jnp
from jax import lax
from jax.experimental import pallas as pl
from jax.experimental.pallas import tpu as pltpu
from jax.sharding import PartitionSpec as P

MESH = pl.DeviceIdType.MESH
epsilon = 1e-06
DP = 32
EX = 16
CAP = 10
RB = 16
LANE = 128
F32 = jnp.float32
BF16 = jnp.bfloat16


def by_rows(left, right):
    return lax.dot_general(left, right, (((1,), (1,)), ((), ())), preferred_element_type=F32)


def by_columns(left, right):
    return lax.dot_general(left, right, (((0,), (0,)), ((), ())), preferred_element_type=F32)


def iota(shape, dim):
    return lax.broadcasted_iota(jnp.int32, shape, dim)


def silu(v):
    return v / (1.0 + jnp.exp(-v))


def loop(start, stop, body):
    def step(j, carry):
        body(j)
        return carry

    lax.fori_loop(start, stop, step, 0)


def layer_kernel(
    res_in, attn, w_in, gain, sh_gate_in, sh_up_in, sh_down_in, ex_gate_in, ex_up_in, ex_down,
    ids, weights,
    out,
    sh_gate, sh_up, sh_down, ex_gate, ex_up,
    w_all, part, rs_buf, res_all, xs, xr, x_own, x_all, a_all, d_all, s_part, s_buf, ys, yr,
    halves, half_in, pack, unpack, sel, comb,
    in_sem, w_send, w_recv, d_send, d_recv, r_send, r_recv, g_send, g_recv, x_send, x_recv,
    xa_send, xa_recv, s_send, s_recv, aa_send, aa_recv, y_send, y_recv, p_send, p_recv,
    h_send, h_recv,
):
    d = lax.axis_index("dp")
    e = lax.axis_index("expert")
    rows = res_in.shape[0]
    hidden = ex_gate.shape[1]
    core = e % 2
    chip = e // 2
    sibling = e + 1 - 2 * core
    z = d % 16
    half = d // 16
    packed = 16 * CAP
    slots = 16 * RB

    def rcopy(src, dst, send, recv, device):
        return pltpu.make_async_remote_copy(
            src_ref=src, dst_ref=dst, send_sem=send, recv_sem=recv,
            device_id=device, device_id_type=MESH,
        )

    def arrival(ref, recv, send, device):
        rcopy(ref, ref, send, recv, device).wait_recv()

    barrier = pltpu.get_barrier_semaphore()

    def greet_dp(j):
        pl.semaphore_signal(barrier, inc=1, device_id=((d + j) % DP, e), device_id_type=MESH)

    def greet_expert(j):
        pl.semaphore_signal(barrier, inc=1, device_id=(d, (e + j) % EX), device_id_type=MESH)

    loop(1, DP, greet_dp)
    loop(1, EX, greet_expert)

    def own_columns(other):
        return ex_down.at[
            other % 2, :, pl.ds(pl.multiple_of((other // 2) * 2 * LANE, 2 * LANE), 2 * LANE)
        ]

    loads = [
        pltpu.make_async_copy(src, dst, in_sem.at[n])
        for n, (src, dst) in enumerate(
            [
                (sh_gate_in, sh_gate), (sh_up_in, sh_up), (sh_down_in, sh_down),
                (ex_gate_in.at[core], ex_gate.at[core]), (ex_up_in.at[core], ex_up.at[core]),
                (own_columns(e), d_all.at[e]),
            ]
        )
    ]
    for copy in loads:
        copy.start()
    w_all[d] = w_in[...]
    experts_iota = iota((64, rows), 0)
    named = jnp.zeros((64, rows), F32)
    for k in range(ids.shape[0]):
        named = named + (ids[k : k + 1, :] == experts_iota).astype(F32)
    upper = (iota((rows, rows), 0) < iota((rows, rows), 1)).astype(F32)
    earlier = jnp.dot(named, upper, preferred_element_type=F32)
    sel_iota = iota((4 * slots, rows), 0).astype(F32)
    comb_iota = iota((2 * slots, rows), 0).astype(F32)
    sel_sum = jnp.zeros((4 * slots, rows), F32)
    comb_sum = jnp.zeros((2 * slots, rows), F32)
    for k in range(ids.shape[0]):
        own = ids[k : k + 1, :]
        place = jnp.sum(jnp.where(own == experts_iota, earlier, 0.0), axis=0, keepdims=True)
        own_z = (own >> 1) & 15
        far = (own >> 5) + half - 2 * (own >> 5) * half
        slot = (far * 2 * slots + own_z * 2 * RB + (own & 1) * RB).astype(F32) + place
        sel_sum = sel_sum + jnp.where(sel_iota == slot, 1.0, 0.0)
        mine = (far * slots + own_z * RB).astype(F32) + place
        mine = jnp.where((own & 1) == core, mine, -1.0)
        comb_sum = comb_sum + jnp.where(comb_iota == mine, weights[k : k + 1, :], 0.0)
    sel[...] = sel_sum.astype(BF16)
    comb[...] = comb_sum

    def packed_row(j):
        inner = j & (RB - 1)
        return jnp.where(inner < CAP, (j >> 4) * CAP + inner, -1)

    pack[...] = (
        packed_row(iota((1, slots), 1)) == iota((packed, slots), 0)
    ).astype(F32).astype(BF16)
    unpack[...] = (
        packed_row(iota((slots, 1), 0)) == iota((slots, packed), 1)
    ).astype(F32).astype(BF16)

    pl.semaphore_wait(barrier, DP - 1 + EX - 1)

    row = d - z
    kind = z % 4
    group = (d // 16) * 4 + z // 4
    above = row + (z + 1) % 16
    below = row + (z + 15) % 16

    def member(q, of):
        return (q // 4) * 16 + (q % 4) * 4 + of

    def w_copy(src, n, device):
        return rcopy(w_all.at[src], w_all.at[src], w_send.at[n], w_recv.at[src], (device, e))

    loop(1, 8, lambda j: rcopy(
        w_in, w_all.at[d], w_send.at[j], w_recv.at[d], (member((group + j) % 8, kind), e)
    ).start())
    for n, device in ((8, above), (9, below)):
        rcopy(w_in, w_all.at[d], w_send.at[n], w_recv.at[d], (device, e)).start()

    def down_copy(j):
        other = (e + j) % EX
        return rcopy(own_columns(other), d_all.at[e], d_send.at[j], d_recv.at[e], (d, other))

    def swap(n, src, dst):
        return rcopy(
            src.at[1 - core], dst.at[core], p_send.at[n], p_recv.at[n], (d, sibling)
        )

    swap(0, ex_gate_in, ex_gate).start()
    swap(1, ex_up_in, ex_up).start()
    loop(1, EX, lambda j: down_copy(j).start())

    def w_arrival(src, device):
        arrival(w_all.at[src], w_recv.at[src], w_send.at[0], (device, e))

    def far_arrival(j):
        src = member((group + 8 - j) % 8, kind)
        w_arrival(src, src)
        w_copy(src, 8 + 2 * j, above).start()
        w_copy(src, 9 + 2 * j, below).start()

    loop(1, 8, far_arrival)

    def near_low(q):
        src = member(q, (kind + 3) % 4)
        w_arrival(src, below)
        w_copy(src, 24 + q, above).start()
        w_arrival(member(q, (kind + 1) % 4), above)

    def near_high(q):
        src = member(q, (kind + 1) % 4)
        w_arrival(src, above)
        w_copy(src, 24 + q, below).start()
        w_arrival(member(q, (kind + 3) % 4), below)

    loop(0, 4, near_low)
    loop(4, 8, near_high)
    loop(0, 4, lambda q: w_arrival(member(q, (kind + 2) % 4), below))
    loop(4, 8, lambda q: w_arrival(member(q, (kind + 2) % 4), above))

    head = by_rows(attn[...], w_all[...].reshape(DP * w_all.shape[1], LANE))
    for i in range(EX):
        part[i] = head[:, i * LANE : (i + 1) * LANE]

    def direct(src, dst, send, recv, j):
        other = (e + j) % EX
        return rcopy(src.at[other], dst.at[e], send.at[j], recv.at[e], (d, other))

    def direct_arrival(dst, send, recv, j):
        src = (e + EX - j) % EX
        arrival(dst.at[src], recv.at[src], send.at[0], (d, src))

    loop(1, EX, lambda j: direct(part, rs_buf, r_send, r_recv, j).start())
    rs_buf[e] = part[e]
    loop(1, EX, lambda j: direct_arrival(rs_buf, r_send, r_recv, j))
    residual = res_in[...].astype(F32) + jnp.sum(rs_buf[...], axis=0)
    res_all[e] = residual

    def res_copy(j):
        other = (e + j) % EX
        return rcopy(res_all.at[e], res_all.at[e], g_send.at[j], g_recv.at[e], (d, other))

    loop(1, EX, lambda j: res_copy(j).start())
    loop(1, EX, lambda j: direct_arrival(res_all, g_send, g_recv, j))

    squares = jnp.zeros((rows, LANE), F32)
    for i in range(EX):
        squares = squares + res_all[i] * res_all[i]
    mean = jnp.sum(squares, axis=1, keepdims=True) / (EX * LANE)
    inverse_rms = lax.rsqrt(mean + epsilon)

    normed_own = (residual * inverse_rms * gain[pl.ds(e, 1), :]).astype(BF16)

    def over_dp(src, dst, h, send, recv, j):
        zz = (z + j) % 16
        other = ((half + h) % 2) * 16 + zz
        return rcopy(src.at[h, zz], dst.at[h, z], send.at[h, j], recv.at[h, z], (other, e))

    def dp_arrivals(dst, h, send, recv):
        def one(j):
            zz = (z + 16 - j) % 16
            other = ((half + h) % 2) * 16 + zz
            arrival(dst.at[h, zz], recv.at[h, zz], send.at[h, 0], (other, e))

        loop(1 - h, 16, one)

    for h in range(2):
        xs[h] = (
            jnp.dot(
                sel[h * 2 * slots : (h + 1) * 2 * slots, :], normed_own,
                preferred_element_type=F32,
            ).astype(BF16).reshape(16, 2, RB, LANE)
        )
        loop(1 - h, 16, lambda j: over_dp(xs, xr, h, x_send, x_recv, j).start())
    xr[0, z] = xs[0, z]

    for copy in loads:
        copy.wait()
    normed = jnp.concatenate(
        [(res_all[i] * inverse_rms * gain[i : i + 1, :]).astype(BF16) for i in range(EX)],
        axis=1,
    )
    shared_active = (
        silu(by_rows(normed, sh_gate[...])) * by_rows(normed, sh_up[...])
    ).astype(BF16)
    shared = jnp.dot(shared_active, sh_down[...], preferred_element_type=F32)
    for i in range(EX):
        s_part[i] = shared[:, i * LANE : (i + 1) * LANE]
    s_buf[e] = s_part[e]

    def x_copy(h, l, j):
        other = ((chip + j) % 8) * 2 + l
        return rcopy(
            x_own.at[h, l], x_all.at[h, e], xa_send.at[h, l * 8 + j], xa_recv.at[h, e],
            (d, other),
        )

    def x_swap(h):
        return rcopy(
            x_own.at[h, 1 - core], x_all.at[h, e], xa_send.at[h, 0], xa_recv.at[h, e],
            (d, sibling),
        )

    def take_rows(h):
        dp_arrivals(xr, h, x_send, x_recv)
        for l in range(2):
            x_own[h, l] = jnp.dot(
                pack[...], xr[h, :, l].reshape(slots, LANE), preferred_element_type=F32
            ).astype(BF16)

        def send(j):
            for l in range(2):
                x_copy(h, l, j).start()

        loop(1, 8, send)
        x_swap(h).start()
        x_all[h, e] = x_own[h, core]

    def a_copy(h, j):
        other = ((chip + j) % 8) * 2 + core
        return rcopy(
            a_all.at[h, chip], a_all.at[h, chip], aa_send.at[h, j], aa_recv.at[h, chip],
            (d, other),
        )

    def activate(h):
        def x_arrival(j):
            src = (e + EX - j) % EX
            arrival(x_all.at[h, src], xa_recv.at[h, src], xa_send.at[h, 0], (d, src))

        loop(1, EX, x_arrival)
        tokens = jnp.concatenate([x_all[h, i] for i in range(EX)], axis=1)
        for b in range(2):
            a_all[h, chip, b] = (
                silu(by_rows(tokens, ex_gate[b])) * by_rows(tokens, ex_up[b])
            ).astype(BF16)
        loop(1, 8, lambda j: a_copy(h, j).start())

    def send_back(h):
        def a_arrival(j):
            src = (chip + 8 - j) % 8
            arrival(
                a_all.at[h, src], aa_recv.at[h, src], aa_send.at[h, 0], (d, src * 2 + core)
            )

        loop(1, 8, a_arrival)
        y_rows = jnp.zeros((packed, 2 * LANE), F32)
        for i in range(EX):
            y_rows = y_rows + jnp.dot(
                a_all[h, i // 2, i % 2], d_all[i], preferred_element_type=F32
            )
        ys[h] = (
            jnp.dot(unpack[...], y_rows.astype(BF16), preferred_element_type=F32)
            .astype(BF16)
            .reshape(16, RB, 2 * LANE)
        )
        loop(1 - h, 16, lambda j: over_dp(ys, yr, h, y_send, y_recv, j).start())

    def collect(h):
        dp_arrivals(yr, h, y_send, y_recv)
        return lax.dot_general(
            comb[h * slots : (h + 1) * slots, :],
            yr[h].reshape(slots, 2 * LANE).astype(F32),
            (((0,), (0,)), ((), ())),
            precision=lax.Precision.HIGHEST, preferred_element_type=F32,
        )

    take_rows(0)
    take_rows(1)
    arrival(ex_gate.at[1 - core], p_recv.at[0], p_send.at[0], (d, sibling))
    arrival(ex_up.at[1 - core], p_recv.at[1], p_send.at[1], (d, sibling))
    activate(0)
    activate(1)
    loop(1, EX, lambda j: direct_arrival(d_all, d_send, d_recv, j))
    send_back(0)
    yr[0, z] = ys[0, z]
    send_back(1)
    loop(1, EX, lambda j: direct(s_part, s_buf, s_send, s_recv, j).start())
    routed = collect(0)
    loop(1, EX, lambda j: direct_arrival(s_buf, s_send, s_recv, j))
    base = residual + jnp.sum(s_buf[...], axis=0)
    routed = routed + collect(1)
    halves[0] = routed[:, :LANE]
    halves[1] = routed[:, LANE:]
    last = rcopy(halves.at[1 - core], half_in, h_send, h_recv, (d, sibling))
    last.start()
    base = base + halves[core]
    last.wait_recv()
    out[...] = (base + half_in[...]).astype(BF16)
    last.wait_send()

    loop(1, 32, lambda n: w_copy(d, n, above).wait_send())
    loop(1, EX, lambda j: down_copy(j).wait_send())
    loop(1, EX, lambda j: direct(part, rs_buf, r_send, r_recv, j).wait_send())
    loop(1, EX, lambda j: direct(s_part, s_buf, s_send, s_recv, j).wait_send())
    loop(1, EX, lambda j: res_copy(j).wait_send())
    swap(0, ex_gate_in, ex_gate).wait_send()
    swap(1, ex_up_in, ex_up).wait_send()
    for h in range(2):
        loop(1 - h, 16, lambda j: over_dp(xs, xr, h, x_send, x_recv, j).wait_send())
        loop(1 - h, 16, lambda j: over_dp(ys, yr, h, y_send, y_recv, j).wait_send())
        loop(1, 8, lambda j: x_copy(h, 0, j).wait_send())
        loop(1, 8, lambda j: x_copy(h, 1, j).wait_send())
        x_swap(h).wait_send()
        loop(1, 8, lambda j: a_copy(h, j).wait_send())


def shards(
    residual_in, attention_values, out_weight, norm_gain, shared_gate, shared_up, shared_down,
    expert_gate, expert_up, expert_down, expert_ids, gate_weights,
):
    rows = residual_in.shape[0]
    local, hidden, width = expert_gate.shape
    packed = 16 * CAP
    vmem = pl.BlockSpec(memory_space=pltpu.VMEM)
    hbm = pl.BlockSpec(memory_space=pl.ANY)

    def sems(*shape):
        return [pltpu.SemaphoreType.DMA(shape)] * 2

    def like(array):
        return pltpu.VMEM(array.shape, array.dtype)

    return pl.pallas_call(
        layer_kernel,
        out_shape=jax.ShapeDtypeStruct((rows, LANE), BF16),
        in_specs=[vmem] * 4 + [hbm] * 6 + [vmem] * 2,
        out_specs=vmem,
        scratch_shapes=[
            like(shared_gate), like(shared_up), like(shared_down), like(expert_gate),
            like(expert_up),
            pltpu.VMEM((DP, width // DP, LANE), BF16),
            pltpu.VMEM((EX, rows, LANE), F32),
            pltpu.VMEM((EX, rows, LANE), F32),
            pltpu.VMEM((EX, rows, LANE), F32),
            pltpu.VMEM((2, 16, 2, RB, LANE), BF16),
            pltpu.VMEM((2, 16, 2, RB, LANE), BF16),
            pltpu.VMEM((2, 2, packed, LANE), BF16),
            pltpu.VMEM((2, EX, packed, LANE), BF16),
            pltpu.VMEM((2, 8, 2, packed, hidden), BF16),
            pltpu.VMEM((EX, hidden, 2 * LANE), BF16),
            pltpu.VMEM((EX, rows, LANE), F32),
            pltpu.VMEM((EX, rows, LANE), F32),
            pltpu.VMEM((2, 16, RB, 2 * LANE), BF16),
            pltpu.VMEM((2, 16, RB, 2 * LANE), BF16),
            pltpu.VMEM((2, rows, LANE), F32),
            pltpu.VMEM((rows, LANE), F32),
            pltpu.VMEM((packed, 16 * RB), BF16),
            pltpu.VMEM((16 * RB, packed), BF16),
            pltpu.VMEM((64 * RB, rows), BF16),
            pltpu.VMEM((32 * RB, rows), F32),
            pltpu.SemaphoreType.DMA((6,)),
        ]
        + sems(DP) + sems(EX) + sems(EX) + sems(EX) + sems(2, 16)
        + sems(2, EX) + sems(EX) + sems(2, 8) + sems(2, 16) + sems(2) + sems(),
        compiler_params=pltpu.CompilerParams(
            collective_id=0, has_side_effects=True, vmem_limit_bytes=60 * 1024 * 1024
        ),
        name="layer",
    )(
        residual_in, attention_values, out_weight.T, norm_gain.reshape(EX, LANE),
        shared_gate, shared_up, shared_down, expert_gate, expert_up, expert_down,
        expert_ids.T, gate_weights.T,
    )


def solution(mesh):
    return jax.shard_map(
        shards,
        mesh=mesh,
        in_specs=(
            P("dp", "expert"),
            P("dp", "expert"),
            P("expert", "dp"),
            P(),
            P("expert", None),
            P("expert", None),
            P("expert", None),
            P("dp", "expert", None),
            P("dp", "expert", None),
            P("dp", "expert", None),
            P("dp", None),
            P("dp", None),
        ),
        out_specs=P("dp", "expert"),
        check_vma=False,
    )
```

```python
import jax
import jax.numpy as jnp
from jax import lax
from jax.experimental import pallas as pl
from jax.experimental.pallas import tpu as pltpu
from jax.sharding import PartitionSpec as P

MESH = pl.DeviceIdType.MESH
epsilon = 1e-06
DP = 32
EX = 16
CAP = 10
RB = 16
LANE = 128
F32 = jnp.float32
BF16 = jnp.bfloat16


def by_rows(left, right):
    return lax.dot_general(left, right, (((1,), (1,)), ((), ())), preferred_element_type=F32)


def by_columns(left, right):
    return lax.dot_general(left, right, (((0,), (0,)), ((), ())), preferred_element_type=F32)


def iota(shape, dim):
    return lax.broadcasted_iota(jnp.int32, shape, dim)


def silu(v):
    return v / (1.0 + jnp.exp(-v))


def loop(start, stop, body):
    def step(j, carry):
        body(j)
        return carry

    lax.fori_loop(start, stop, step, 0)


def layer_kernel(
    res_in, attn, w_in, gain, sh_gate_in, sh_up_in, sh_down_in, ex_gate_in, ex_up_in, ex_down,
    ids, weights,
    out,
    sh_gate, sh_up, sh_down, ex_gate, ex_up,
    w_all, part, rs_buf, sq_all, n_all, xs, xr, x_own, x_all, a_all, d_all, s_part, s_buf, ys, yr,
    halves, half_in, pack, unpack, sel, comb,
    in_sem, w_send, w_recv, d_send, d_recv, r_send, r_recv, q_send, q_recv, g_send, g_recv, x_send, x_recv,
    xa_send, xa_recv, s_send, s_recv, aa_send, aa_recv, y_send, y_recv, p_send, p_recv,
    h_send, h_recv,
):
    d = lax.axis_index("dp")
    e = lax.axis_index("expert")
    rows = res_in.shape[0]
    hidden = ex_gate.shape[1]
    core = e % 2
    chip = e // 2
    sibling = e + 1 - 2 * core
    z = d % 16
    half = d // 16
    packed = 16 * CAP
    slots = 16 * RB

    def rcopy(src, dst, send, recv, device):
        return pltpu.make_async_remote_copy(
            src_ref=src, dst_ref=dst, send_sem=send, recv_sem=recv,
            device_id=device, device_id_type=MESH,
        )

    def arrival(ref, recv, send, device):
        rcopy(ref, ref, send, recv, device).wait_recv()

    barrier = pltpu.get_barrier_semaphore()

    def greet_dp(j):
        pl.semaphore_signal(barrier, inc=1, device_id=((d + j) % DP, e), device_id_type=MESH)

    def greet_expert(j):
        pl.semaphore_signal(barrier, inc=1, device_id=(d, (e + j) % EX), device_id_type=MESH)

    loop(1, DP, greet_dp)
    loop(1, EX, greet_expert)

    def own_columns(other):
        return ex_down.at[
            other % 2, :, pl.ds(pl.multiple_of((other // 2) * 2 * LANE, 2 * LANE), 2 * LANE)
        ]

    loads = [
        pltpu.make_async_copy(src, dst, in_sem.at[n])
        for n, (src, dst) in enumerate(
            [
                (sh_gate_in, sh_gate), (sh_up_in, sh_up), (sh_down_in, sh_down),
                (ex_gate_in.at[core], ex_gate.at[core]), (ex_up_in.at[core], ex_up.at[core]),
                (own_columns(e), d_all.at[e]),
            ]
        )
    ]
    for copy in loads:
        copy.start()
    w_all[d] = w_in[...]
    experts_iota = iota((64, rows), 0)
    named = jnp.zeros((64, rows), F32)
    for k in range(ids.shape[0]):
        named = named + (ids[k : k + 1, :] == experts_iota).astype(F32)
    upper = (iota((rows, rows), 0) < iota((rows, rows), 1)).astype(F32)
    earlier = jnp.dot(named, upper, preferred_element_type=F32)
    sel_iota = iota((4 * slots, rows), 0).astype(F32)
    comb_iota = iota((2 * slots, rows), 0).astype(F32)
    sel_sum = jnp.zeros((4 * slots, rows), F32)
    comb_sum = jnp.zeros((2 * slots, rows), F32)
    for k in range(ids.shape[0]):
        own = ids[k : k + 1, :]
        place = jnp.sum(jnp.where(own == experts_iota, earlier, 0.0), axis=0, keepdims=True)
        own_z = (own >> 1) & 15
        far = (own >> 5) + half - 2 * (own >> 5) * half
        slot = (far * 2 * slots + own_z * 2 * RB + (own & 1) * RB).astype(F32) + place
        sel_sum = sel_sum + jnp.where(sel_iota == slot, 1.0, 0.0)
        mine = (far * slots + own_z * RB).astype(F32) + place
        mine = jnp.where((own & 1) == core, mine, -1.0)
        comb_sum = comb_sum + jnp.where(comb_iota == mine, weights[k : k + 1, :], 0.0)
    sel[...] = sel_sum.astype(BF16)
    comb[...] = comb_sum

    def packed_row(j):
        inner = j & (RB - 1)
        return jnp.where(inner < CAP, (j >> 4) * CAP + inner, -1)

    pack[...] = (
        packed_row(iota((1, slots), 1)) == iota((packed, slots), 0)
    ).astype(F32).astype(BF16)
    unpack[...] = (
        packed_row(iota((slots, 1), 0)) == iota((slots, packed), 1)
    ).astype(F32).astype(BF16)

    pl.semaphore_wait(barrier, DP - 1 + EX - 1)

    row = d - z
    kind = z % 4
    group = (d // 16) * 4 + z // 4
    above = row + (z + 1) % 16
    below = row + (z + 15) % 16

    def member(q, of):
        return (q // 4) * 16 + (q % 4) * 4 + of

    def w_copy(src, n, device):
        return rcopy(w_all.at[src], w_all.at[src], w_send.at[n], w_recv.at[src], (device, e))

    loop(1, 8, lambda j: rcopy(
        w_in, w_all.at[d], w_send.at[j], w_recv.at[d], (member((group + j) % 8, kind), e)
    ).start())
    for n, device in ((8, above), (9, below)):
        rcopy(w_in, w_all.at[d], w_send.at[n], w_recv.at[d], (device, e)).start()

    def down_copy(j):
        other = (e + j) % EX
        return rcopy(own_columns(other), d_all.at[e], d_send.at[j], d_recv.at[e], (d, other))

    def swap(n, src, dst):
        return rcopy(
            src.at[1 - core], dst.at[core], p_send.at[n], p_recv.at[n], (d, sibling)
        )

    def w_arrival(src, device):
        arrival(w_all.at[src], w_recv.at[src], w_send.at[0], (device, e))

    def far_arrival(j):
        src = member((group + 8 - j) % 8, kind)
        w_arrival(src, src)
        w_copy(src, 8 + 2 * j, above).start()
        w_copy(src, 9 + 2 * j, below).start()

    loop(1, 8, far_arrival)
    loop(1, EX, lambda j: down_copy(j).start())
    swap(0, ex_gate_in, ex_gate).start()
    swap(1, ex_up_in, ex_up).start()

    def near_low(q):
        src = member(q, (kind + 3) % 4)
        w_arrival(src, below)
        w_copy(src, 24 + q, above).start()
        w_arrival(member(q, (kind + 1) % 4), above)

    def near_high(q):
        src = member(q, (kind + 1) % 4)
        w_arrival(src, above)
        w_copy(src, 24 + q, below).start()
        w_arrival(member(q, (kind + 3) % 4), below)

    loop(0, 4, near_low)
    loop(4, 8, near_high)
    loop(0, 4, lambda q: w_arrival(member(q, (kind + 2) % 4), below))
    loop(4, 8, lambda q: w_arrival(member(q, (kind + 2) % 4), above))

    head = by_rows(attn[...], w_all[...].reshape(DP * w_all.shape[1], LANE))
    for i in range(EX):
        part[i] = head[:, i * LANE : (i + 1) * LANE]

    def direct(src, dst, send, recv, j):
        other = (e + j) % EX
        return rcopy(src.at[other], dst.at[e], send.at[j], recv.at[e], (d, other))

    def direct_arrival(dst, send, recv, j):
        src = (e + EX - j) % EX
        arrival(dst.at[src], recv.at[src], send.at[0], (d, src))

    loop(1, EX, lambda j: direct(part, rs_buf, r_send, r_recv, j).start())
    rs_buf[e] = part[e]
    loop(1, EX, lambda j: direct_arrival(rs_buf, r_send, r_recv, j))
    residual = res_in[...].astype(F32) + jnp.sum(rs_buf[...], axis=0)
    def to_all(buf, send, recv, j):
        other = (e + j) % EX
        return rcopy(buf.at[e], buf.at[e], send.at[j], recv.at[e], (d, other))

    def exact(left, right, contract):
        return lax.dot_general(
            left, right, (contract, ((), ())),
            precision=lax.Precision.HIGHEST, preferred_element_type=F32,
        )

    sq_all[e] = exact(jnp.ones((8, LANE), F32), residual * residual, ((1,), (1,)))
    loop(1, EX, lambda j: to_all(sq_all, q_send, q_recv, j).start())
    loop(1, EX, lambda j: direct_arrival(sq_all, q_send, q_recv, j))
    squares = jnp.sum(sq_all[...], axis=0)
    mean = exact(squares, jnp.full((8, LANE), 0.125 / (EX * LANE), F32), ((0,), (0,)))
    inverse_rms = lax.rsqrt(mean + epsilon)

    normed_own = (residual * inverse_rms * gain[pl.ds(e, 1), :]).astype(BF16)
    n_all[e] = normed_own

    def over_dp(src, dst, h, send, recv, j):
        zz = (z + j) % 16
        other = ((half + h) % 2) * 16 + zz
        return rcopy(src.at[h, zz], dst.at[h, z], send.at[h, j], recv.at[h, z], (other, e))

    def dp_arrivals(dst, h, send, recv):
        def one(j):
            zz = (z + 16 - j) % 16
            other = ((half + h) % 2) * 16 + zz
            arrival(dst.at[h, zz], recv.at[h, zz], send.at[h, 0], (other, e))

        loop(1 - h, 16, one)

    for h in range(2):
        xs[h] = (
            jnp.dot(
                sel[h * 2 * slots : (h + 1) * 2 * slots, :], normed_own,
                preferred_element_type=F32,
            ).astype(BF16).reshape(16, 2, RB, LANE)
        )
        loop(1 - h, 16, lambda j: over_dp(xs, xr, h, x_send, x_recv, j).start())
    xr[0, z] = xs[0, z]
    loop(1, EX, lambda j: to_all(n_all, g_send, g_recv, j).start())

    for copy in loads:
        copy.wait()
    loop(1, EX, lambda j: direct_arrival(n_all, g_send, g_recv, j))
    normed = jnp.concatenate([n_all[i] for i in range(EX)], axis=1)
    shared_active = (
        silu(by_rows(normed, sh_gate[...])) * by_rows(normed, sh_up[...])
    ).astype(BF16)
    shared = jnp.dot(shared_active, sh_down[...], preferred_element_type=F32)
    for i in range(EX):
        s_part[i] = shared[:, i * LANE : (i + 1) * LANE]
    s_buf[e] = s_part[e]

    def x_copy(h, l, j):
        other = ((chip + j) % 8) * 2 + l
        return rcopy(
            x_own.at[h, l], x_all.at[h, e], xa_send.at[h, l * 8 + j], xa_recv.at[h, e],
            (d, other),
        )

    def x_swap(h):
        return rcopy(
            x_own.at[h, 1 - core], x_all.at[h, e], xa_send.at[h, 0], xa_recv.at[h, e],
            (d, sibling),
        )

    def take_rows(h):
        dp_arrivals(xr, h, x_send, x_recv)
        for l in range(2):
            x_own[h, l] = jnp.dot(
                pack[...], xr[h, :, l].reshape(slots, LANE), preferred_element_type=F32
            ).astype(BF16)

        def send(j):
            for l in range(2):
                x_copy(h, l, j).start()

        loop(1, 8, send)
        x_swap(h).start()
        x_all[h, e] = x_own[h, core]

    def a_copy(h, j):
        other = ((chip + j) % 8) * 2 + core
        return rcopy(
            a_all.at[h, chip], a_all.at[h, chip], aa_send.at[h, j], aa_recv.at[h, chip],
            (d, other),
        )

    def activate(h):
        def x_arrival(j):
            src = (e + EX - j) % EX
            arrival(x_all.at[h, src], xa_recv.at[h, src], xa_send.at[h, 0], (d, src))

        loop(1, EX, x_arrival)
        tokens = jnp.concatenate([x_all[h, i] for i in range(EX)], axis=1)
        for b in range(2):
            a_all[h, chip, b] = (
                silu(by_rows(tokens, ex_gate[b])) * by_rows(tokens, ex_up[b])
            ).astype(BF16)
        loop(1, 8, lambda j: a_copy(h, j).start())

    def send_back(h):
        def a_arrival(j):
            src = (chip + 8 - j) % 8
            arrival(
                a_all.at[h, src], aa_recv.at[h, src], aa_send.at[h, 0], (d, src * 2 + core)
            )

        loop(1, 8, a_arrival)
        y_rows = jnp.zeros((packed, 2 * LANE), F32)
        for i in range(EX):
            y_rows = y_rows + jnp.dot(
                a_all[h, i // 2, i % 2], d_all[i], preferred_element_type=F32
            )
        ys[h] = (
            jnp.dot(unpack[...], y_rows.astype(BF16), preferred_element_type=F32)
            .astype(BF16)
            .reshape(16, RB, 2 * LANE)
        )
        loop(1 - h, 16, lambda j: over_dp(ys, yr, h, y_send, y_recv, j).start())

    def collect(h):
        dp_arrivals(yr, h, y_send, y_recv)
        return lax.dot_general(
            comb[h * slots : (h + 1) * slots, :],
            yr[h].reshape(slots, 2 * LANE).astype(F32),
            (((0,), (0,)), ((), ())),
            precision=lax.Precision.HIGHEST, preferred_element_type=F32,
        )

    take_rows(0)
    take_rows(1)
    arrival(ex_gate.at[1 - core], p_recv.at[0], p_send.at[0], (d, sibling))
    arrival(ex_up.at[1 - core], p_recv.at[1], p_send.at[1], (d, sibling))
    activate(0)
    activate(1)
    loop(1, EX, lambda j: direct_arrival(d_all, d_send, d_recv, j))
    send_back(0)
    yr[0, z] = ys[0, z]
    send_back(1)
    loop(1, EX, lambda j: direct(s_part, s_buf, s_send, s_recv, j).start())
    routed = collect(0)
    loop(1, EX, lambda j: direct_arrival(s_buf, s_send, s_recv, j))
    base = residual + jnp.sum(s_buf[...], axis=0)
    routed = routed + collect(1)
    halves[0] = routed[:, :LANE]
    halves[1] = routed[:, LANE:]
    last = rcopy(halves.at[1 - core], half_in, h_send, h_recv, (d, sibling))
    last.start()
    base = base + halves[core]
    last.wait_recv()
    out[...] = (base + half_in[...]).astype(BF16)
    last.wait_send()

    loop(1, 32, lambda n: w_copy(d, n, above).wait_send())
    loop(1, EX, lambda j: down_copy(j).wait_send())
    loop(1, EX, lambda j: direct(part, rs_buf, r_send, r_recv, j).wait_send())
    loop(1, EX, lambda j: direct(s_part, s_buf, s_send, s_recv, j).wait_send())
    loop(1, EX, lambda j: to_all(sq_all, q_send, q_recv, j).wait_send())
    loop(1, EX, lambda j: to_all(n_all, g_send, g_recv, j).wait_send())
    swap(0, ex_gate_in, ex_gate).wait_send()
    swap(1, ex_up_in, ex_up).wait_send()
    for h in range(2):
        loop(1 - h, 16, lambda j: over_dp(xs, xr, h, x_send, x_recv, j).wait_send())
        loop(1 - h, 16, lambda j: over_dp(ys, yr, h, y_send, y_recv, j).wait_send())
        loop(1, 8, lambda j: x_copy(h, 0, j).wait_send())
        loop(1, 8, lambda j: x_copy(h, 1, j).wait_send())
        x_swap(h).wait_send()
        loop(1, 8, lambda j: a_copy(h, j).wait_send())


def shards(
    residual_in, attention_values, out_weight, norm_gain, shared_gate, shared_up, shared_down,
    expert_gate, expert_up, expert_down, expert_ids, gate_weights,
):
    rows = residual_in.shape[0]
    local, hidden, width = expert_gate.shape
    packed = 16 * CAP
    vmem = pl.BlockSpec(memory_space=pltpu.VMEM)
    hbm = pl.BlockSpec(memory_space=pl.ANY)

    def sems(*shape):
        return [pltpu.SemaphoreType.DMA(shape)] * 2

    def like(array):
        return pltpu.VMEM(array.shape, array.dtype)

    return pl.pallas_call(
        layer_kernel,
        out_shape=jax.ShapeDtypeStruct((rows, LANE), BF16),
        in_specs=[vmem] * 4 + [hbm] * 6 + [vmem] * 2,
        out_specs=vmem,
        scratch_shapes=[
            like(shared_gate), like(shared_up), like(shared_down), like(expert_gate),
            like(expert_up),
            pltpu.VMEM((DP, width // DP, LANE), BF16),
            pltpu.VMEM((EX, rows, LANE), F32),
            pltpu.VMEM((EX, rows, LANE), F32),
            pltpu.VMEM((EX, 8, rows), F32),
            pltpu.VMEM((EX, rows, LANE), BF16),
            pltpu.VMEM((2, 16, 2, RB, LANE), BF16),
            pltpu.VMEM((2, 16, 2, RB, LANE), BF16),
            pltpu.VMEM((2, 2, packed, LANE), BF16),
            pltpu.VMEM((2, EX, packed, LANE), BF16),
            pltpu.VMEM((2, 8, 2, packed, hidden), BF16),
            pltpu.VMEM((EX, hidden, 2 * LANE), BF16),
            pltpu.VMEM((EX, rows, LANE), F32),
            pltpu.VMEM((EX, rows, LANE), F32),
            pltpu.VMEM((2, 16, RB, 2 * LANE), BF16),
            pltpu.VMEM((2, 16, RB, 2 * LANE), BF16),
            pltpu.VMEM((2, rows, LANE), F32),
            pltpu.VMEM((rows, LANE), F32),
            pltpu.VMEM((packed, 16 * RB), BF16),
            pltpu.VMEM((16 * RB, packed), BF16),
            pltpu.VMEM((64 * RB, rows), BF16),
            pltpu.VMEM((32 * RB, rows), F32),
            pltpu.SemaphoreType.DMA((6,)),
        ]
        + sems(DP) + sems(EX) + sems(EX) + sems(EX) + sems(EX) + sems(2, 16)
        + sems(2, EX) + sems(EX) + sems(2, 8) + sems(2, 16) + sems(2) + sems(),
        compiler_params=pltpu.CompilerParams(
            collective_id=0, has_side_effects=True, vmem_limit_bytes=60 * 1024 * 1024
        ),
        name="layer",
    )(
        residual_in, attention_values, out_weight.T, norm_gain.reshape(EX, LANE),
        shared_gate, shared_up, shared_down, expert_gate, expert_up, expert_down,
        expert_ids.T, gate_weights.T,
    )


def solution(mesh):
    return jax.shard_map(
        shards,
        mesh=mesh,
        in_specs=(
            P("dp", "expert"),
            P("dp", "expert"),
            P("expert", "dp"),
            P(),
            P("expert", None),
            P("expert", None),
            P("expert", None),
            P("dp", "expert", None),
            P("dp", "expert", None),
            P("dp", "expert", None),
            P("dp", None),
            P("dp", None),
        ),
        out_specs=P("dp", "expert"),
        check_vma=False,
    )
```

```python
import jax
import jax.numpy as jnp
from jax import lax
from jax.experimental import pallas as pl
from jax.experimental.pallas import tpu as pltpu
from jax.sharding import PartitionSpec as P

MESH = pl.DeviceIdType.MESH
epsilon = 1e-06
DP = 32
EX = 16
CAP = 10
RB = 16
LANE = 128
F32 = jnp.float32
BF16 = jnp.bfloat16


def by_rows(left, right):
    return lax.dot_general(left, right, (((1,), (1,)), ((), ())), preferred_element_type=F32)


def by_columns(left, right):
    return lax.dot_general(left, right, (((0,), (0,)), ((), ())), preferred_element_type=F32)


def iota(shape, dim):
    return lax.broadcasted_iota(jnp.int32, shape, dim)


def silu(v):
    return v / (1.0 + jnp.exp(-v))


def loop(start, stop, body):
    def step(j, carry):
        body(j)
        return carry

    lax.fori_loop(start, stop, step, 0)


def layer_kernel(
    res_in, attn, w_in, gain, sh_gate_in, sh_up_in, sh_down_in, ex_gate_in, ex_up_in, ex_down,
    ids, weights,
    out,
    sh_gate, sh_up, sh_down, ex_gate, ex_up,
    w_all, part, rs_buf, sq_all, n_all, xs, xr, x_own, x_all, a_all, d_all, s_part, s_buf, ys, yr,
    halves, half_in, pack, unpack, sel, comb,
    in_sem, w_send, w_recv, d_send, d_recv, r_send, r_recv, q_send, q_recv, g_send, g_recv, x_send, x_recv,
    xa_send, xa_recv, s_send, s_recv, aa_send, aa_recv, y_send, y_recv, p_send, p_recv,
    h_send, h_recv,
):
    d = lax.axis_index("dp")
    e = lax.axis_index("expert")
    rows = res_in.shape[0]
    hidden = ex_gate.shape[1]
    core = e % 2
    chip = e // 2
    sibling = e + 1 - 2 * core
    z = d % 16
    half = d // 16
    packed = 16 * CAP
    slots = 16 * RB

    def rcopy(src, dst, send, recv, device):
        return pltpu.make_async_remote_copy(
            src_ref=src, dst_ref=dst, send_sem=send, recv_sem=recv,
            device_id=device, device_id_type=MESH,
        )

    def arrival(ref, recv, send, device):
        rcopy(ref, ref, send, recv, device).wait_recv()

    barrier = pltpu.get_barrier_semaphore()

    def greet_dp(j):
        pl.semaphore_signal(barrier, inc=1, device_id=((d + j) % DP, e), device_id_type=MESH)

    def greet_expert(j):
        pl.semaphore_signal(barrier, inc=1, device_id=(d, (e + j) % EX), device_id_type=MESH)

    loop(1, DP, greet_dp)
    loop(1, EX, greet_expert)

    def own_columns(other):
        return ex_down.at[
            other % 2, :, pl.ds(pl.multiple_of((other // 2) * 2 * LANE, 2 * LANE), 2 * LANE)
        ]

    loads = [
        pltpu.make_async_copy(src, dst, in_sem.at[n])
        for n, (src, dst) in enumerate(
            [
                (sh_gate_in, sh_gate), (sh_up_in, sh_up), (sh_down_in, sh_down),
                (ex_gate_in.at[core], ex_gate.at[core]), (ex_up_in.at[core], ex_up.at[core]),
                (own_columns(e), d_all.at[e]),
            ]
        )
    ]
    for copy in loads:
        copy.start()
    w_all[d] = w_in[...]
    experts_iota = iota((64, rows), 0)
    named = jnp.zeros((64, rows), F32)
    for k in range(ids.shape[0]):
        named = named + (ids[k : k + 1, :] == experts_iota).astype(F32)
    upper = (iota((rows, rows), 0) < iota((rows, rows), 1)).astype(F32)
    earlier = jnp.dot(named, upper, preferred_element_type=F32)
    sel_iota = iota((4 * slots, rows), 0).astype(F32)
    comb_iota = iota((2 * slots, rows), 0).astype(F32)
    sel_sum = jnp.zeros((4 * slots, rows), F32)
    comb_sum = jnp.zeros((2 * slots, rows), F32)
    for k in range(ids.shape[0]):
        own = ids[k : k + 1, :]
        place = jnp.sum(jnp.where(own == experts_iota, earlier, 0.0), axis=0, keepdims=True)
        own_z = (own >> 1) & 15
        far = (own >> 5) + half - 2 * (own >> 5) * half
        slot = (far * 2 * slots + own_z * 2 * RB + (own & 1) * RB).astype(F32) + place
        sel_sum = sel_sum + jnp.where(sel_iota == slot, 1.0, 0.0)
        mine = (far * slots + own_z * RB).astype(F32) + place
        mine = jnp.where((own & 1) == core, mine, -1.0)
        comb_sum = comb_sum + jnp.where(comb_iota == mine, weights[k : k + 1, :], 0.0)
    sel[...] = sel_sum.astype(BF16)
    comb[...] = comb_sum

    def packed_row(j):
        inner = j & (RB - 1)
        return jnp.where(inner < CAP, (j >> 4) * CAP + inner, -1)

    pack[...] = (
        packed_row(iota((1, slots), 1)) == iota((packed, slots), 0)
    ).astype(F32).astype(BF16)
    unpack[...] = (
        packed_row(iota((slots, 1), 0)) == iota((slots, packed), 1)
    ).astype(F32).astype(BF16)

    pl.semaphore_wait(barrier, DP - 1 + EX - 1)

    row = d - z
    kind = z % 4
    group = (d // 16) * 4 + z // 4
    above = row + (z + 1) % 16
    below = row + (z + 15) % 16

    def member(q, of):
        return (q // 4) * 16 + (q % 4) * 4 + of

    def w_copy(src, n, device):
        return rcopy(w_all.at[src], w_all.at[src], w_send.at[n], w_recv.at[src], (device, e))

    loop(1, 8, lambda j: rcopy(
        w_in, w_all.at[d], w_send.at[j], w_recv.at[d], (member((group + j) % 8, kind), e)
    ).start())
    for n, device in ((8, above), (9, below)):
        rcopy(w_in, w_all.at[d], w_send.at[n], w_recv.at[d], (device, e)).start()

    def down_copy(j):
        other = (e + j) % EX
        return rcopy(own_columns(other), d_all.at[e], d_send.at[j], d_recv.at[e], (d, other))

    def swap(n, src, dst):
        return rcopy(
            src.at[1 - core], dst.at[core], p_send.at[n], p_recv.at[n], (d, sibling)
        )

    def w_arrival(src, device):
        arrival(w_all.at[src], w_recv.at[src], w_send.at[0], (device, e))

    def far_arrival(j):
        src = member((group + 8 - j) % 8, kind)
        w_arrival(src, src)
        w_copy(src, 8 + 2 * j, above).start()
        w_copy(src, 9 + 2 * j, below).start()

    loop(1, 8, far_arrival)
    loop(1, EX, lambda j: down_copy(j).start())
    swap(0, ex_gate_in, ex_gate).start()
    swap(1, ex_up_in, ex_up).start()

    def near_low(q):
        src = member(q, (kind + 3) % 4)
        w_arrival(src, below)
        w_copy(src, 24 + q, above).start()
        w_arrival(member(q, (kind + 1) % 4), above)

    def near_high(q):
        src = member(q, (kind + 1) % 4)
        w_arrival(src, above)
        w_copy(src, 24 + q, below).start()
        w_arrival(member(q, (kind + 3) % 4), below)

    loop(0, 4, near_low)
    loop(4, 8, near_high)
    loop(0, 4, lambda q: w_arrival(member(q, (kind + 2) % 4), below))
    loop(4, 8, lambda q: w_arrival(member(q, (kind + 2) % 4), above))

    head = by_rows(attn[...], w_all[...].reshape(DP * w_all.shape[1], LANE))
    for i in range(EX):
        part[i] = head[:, i * LANE : (i + 1) * LANE]

    def direct(src, dst, send, recv, j):
        other = (e + j) % EX
        return rcopy(src.at[other], dst.at[e], send.at[j], recv.at[e], (d, other))

    def direct_arrival(dst, send, recv, j):
        src = (e + EX - j) % EX
        arrival(dst.at[src], recv.at[src], send.at[0], (d, src))

    loop(1, EX, lambda j: direct(part, rs_buf, r_send, r_recv, j).start())
    rs_buf[e] = part[e]
    loop(1, EX, lambda j: direct_arrival(rs_buf, r_send, r_recv, j))
    residual = res_in[...].astype(F32) + jnp.sum(rs_buf[...], axis=0)
    def to_all(buf, send, recv, j):
        other = (e + j) % EX
        return rcopy(buf.at[e], buf.at[e], send.at[j], recv.at[e], (d, other))

    def exact(left, right, contract):
        return lax.dot_general(
            left, right, (contract, ((), ())),
            precision=lax.Precision.HIGHEST, preferred_element_type=F32,
        )

    sq_all[e] = exact(jnp.ones((8, LANE), F32), residual * residual, ((1,), (1,)))
    loop(1, EX, lambda j: to_all(sq_all, q_send, q_recv, j).start())
    loop(1, EX, lambda j: direct_arrival(sq_all, q_send, q_recv, j))
    squares = jnp.sum(sq_all[...], axis=0)
    mean = exact(squares, jnp.full((8, LANE), 0.125 / (EX * LANE), F32), ((0,), (0,)))
    inverse_rms = lax.rsqrt(mean + epsilon)

    normed_own = (residual * inverse_rms * gain[pl.ds(e, 1), :]).astype(BF16)
    n_all[e] = normed_own

    def far_first(t):
        return (8 + (t // 2) * (1 - 2 * (t % 2))) % 16

    def over_dp(src, dst, h, send, recv, j):
        zz = (z + j) % 16
        other = ((half + h) % 2) * 16 + zz
        return rcopy(src.at[h, zz], dst.at[h, z], send.at[h, j], recv.at[h, z], (other, e))

    def dp_arrivals(dst, h, send, recv):
        def one(j):
            zz = (z + 16 - j) % 16
            other = ((half + h) % 2) * 16 + zz
            arrival(dst.at[h, zz], recv.at[h, zz], send.at[h, 0], (other, e))

        loop(1 - h, 16, one)

    for h in range(2):
        xs[h] = (
            jnp.dot(
                sel[h * 2 * slots : (h + 1) * 2 * slots, :], normed_own,
                preferred_element_type=F32,
            ).astype(BF16).reshape(16, 2, RB, LANE)
        )
        loop(1, 16 + h, lambda t: over_dp(xs, xr, h, x_send, x_recv, far_first(t)).start())
    xr[0, z] = xs[0, z]
    loop(1, EX, lambda j: to_all(n_all, g_send, g_recv, j).start())

    def x_copy(h, l, j):
        other = ((chip + j) % 8) * 2 + l
        return rcopy(
            x_own.at[h, l], x_all.at[h, e], xa_send.at[h, l * 8 + j], xa_recv.at[h, e],
            (d, other),
        )

    def x_swap(h):
        return rcopy(
            x_own.at[h, 1 - core], x_all.at[h, e], xa_send.at[h, 0], xa_recv.at[h, e],
            (d, sibling),
        )

    def take_rows(h):
        dp_arrivals(xr, h, x_send, x_recv)
        for l in range(2):
            x_own[h, l] = jnp.dot(
                pack[...], xr[h, :, l].reshape(slots, LANE), preferred_element_type=F32
            ).astype(BF16)

        def send(j):
            for l in range(2):
                x_copy(h, l, j).start()

        loop(1, 8, send)
        x_swap(h).start()
        x_all[h, e] = x_own[h, core]

    def a_copy(h, j):
        other = ((chip + j) % 8) * 2 + core
        return rcopy(
            a_all.at[h, chip], a_all.at[h, chip], aa_send.at[h, j], aa_recv.at[h, chip],
            (d, other),
        )

    def activate(h):
        def x_arrival(j):
            src = (e + EX - j) % EX
            arrival(x_all.at[h, src], xa_recv.at[h, src], xa_send.at[h, 0], (d, src))

        loop(1, EX, x_arrival)
        tokens = jnp.concatenate([x_all[h, i] for i in range(EX)], axis=1)
        for b in range(2):
            a_all[h, chip, b] = (
                silu(by_rows(tokens, ex_gate[b])) * by_rows(tokens, ex_up[b])
            ).astype(BF16)
        loop(1, 8, lambda j: a_copy(h, j).start())

    def send_back(h):
        def a_arrival(j):
            src = (chip + 8 - j) % 8
            arrival(
                a_all.at[h, src], aa_recv.at[h, src], aa_send.at[h, 0], (d, src * 2 + core)
            )

        loop(1, 8, a_arrival)
        y_rows = jnp.zeros((packed, 2 * LANE), F32)
        for i in range(EX):
            y_rows = y_rows + jnp.dot(
                a_all[h, i // 2, i % 2], d_all[i], preferred_element_type=F32
            )
        ys[h] = (
            jnp.dot(unpack[...], y_rows.astype(BF16), preferred_element_type=F32)
            .astype(BF16)
            .reshape(16, RB, 2 * LANE)
        )
        loop(1, 16 + h, lambda t: over_dp(ys, yr, h, y_send, y_recv, far_first(t)).start())

    def collect(h):
        dp_arrivals(yr, h, y_send, y_recv)
        return lax.dot_general(
            comb[h * slots : (h + 1) * slots, :],
            yr[h].reshape(slots, 2 * LANE).astype(F32),
            (((0,), (0,)), ((), ())),
            precision=lax.Precision.HIGHEST, preferred_element_type=F32,
        )

    take_rows(0)
    take_rows(1)

    for copy in loads:
        copy.wait()
    loop(1, EX, lambda j: direct_arrival(n_all, g_send, g_recv, j))
    normed = jnp.concatenate([n_all[i] for i in range(EX)], axis=1)
    shared_active = (
        silu(by_rows(normed, sh_gate[...])) * by_rows(normed, sh_up[...])
    ).astype(BF16)
    shared = jnp.dot(shared_active, sh_down[...], preferred_element_type=F32)
    for i in range(EX):
        s_part[i] = shared[:, i * LANE : (i + 1) * LANE]
    s_buf[e] = s_part[e]

    arrival(ex_gate.at[1 - core], p_recv.at[0], p_send.at[0], (d, sibling))
    arrival(ex_up.at[1 - core], p_recv.at[1], p_send.at[1], (d, sibling))
    activate(0)
    activate(1)
    loop(1, EX, lambda j: direct_arrival(d_all, d_send, d_recv, j))
    send_back(0)
    yr[0, z] = ys[0, z]
    send_back(1)
    loop(1, EX, lambda j: direct(s_part, s_buf, s_send, s_recv, j).start())
    routed = collect(0)
    loop(1, EX, lambda j: direct_arrival(s_buf, s_send, s_recv, j))
    base = residual + jnp.sum(s_buf[...], axis=0)
    routed = routed + collect(1)
    halves[0] = routed[:, :LANE]
    halves[1] = routed[:, LANE:]
    last = rcopy(halves.at[1 - core], half_in, h_send, h_recv, (d, sibling))
    last.start()
    base = base + halves[core]
    last.wait_recv()
    out[...] = (base + half_in[...]).astype(BF16)
    last.wait_send()

    loop(1, 32, lambda n: w_copy(d, n, above).wait_send())
    loop(1, EX, lambda j: down_copy(j).wait_send())
    loop(1, EX, lambda j: direct(part, rs_buf, r_send, r_recv, j).wait_send())
    loop(1, EX, lambda j: direct(s_part, s_buf, s_send, s_recv, j).wait_send())
    loop(1, EX, lambda j: to_all(sq_all, q_send, q_recv, j).wait_send())
    loop(1, EX, lambda j: to_all(n_all, g_send, g_recv, j).wait_send())
    swap(0, ex_gate_in, ex_gate).wait_send()
    swap(1, ex_up_in, ex_up).wait_send()
    for h in range(2):
        loop(1 - h, 16, lambda j: over_dp(xs, xr, h, x_send, x_recv, j).wait_send())
        loop(1 - h, 16, lambda j: over_dp(ys, yr, h, y_send, y_recv, j).wait_send())
        loop(1, 8, lambda j: x_copy(h, 0, j).wait_send())
        loop(1, 8, lambda j: x_copy(h, 1, j).wait_send())
        x_swap(h).wait_send()
        loop(1, 8, lambda j: a_copy(h, j).wait_send())


def shards(
    residual_in, attention_values, out_weight, norm_gain, shared_gate, shared_up, shared_down,
    expert_gate, expert_up, expert_down, expert_ids, gate_weights,
):
    rows = residual_in.shape[0]
    local, hidden, width = expert_gate.shape
    packed = 16 * CAP
    vmem = pl.BlockSpec(memory_space=pltpu.VMEM)
    hbm = pl.BlockSpec(memory_space=pl.ANY)

    def sems(*shape):
        return [pltpu.SemaphoreType.DMA(shape)] * 2

    def like(array):
        return pltpu.VMEM(array.shape, array.dtype)

    return pl.pallas_call(
        layer_kernel,
        out_shape=jax.ShapeDtypeStruct((rows, LANE), BF16),
        in_specs=[vmem] * 4 + [hbm] * 6 + [vmem] * 2,
        out_specs=vmem,
        scratch_shapes=[
            like(shared_gate), like(shared_up), like(shared_down), like(expert_gate),
            like(expert_up),
            pltpu.VMEM((DP, width // DP, LANE), BF16),
            pltpu.VMEM((EX, rows, LANE), F32),
            pltpu.VMEM((EX, rows, LANE), F32),
            pltpu.VMEM((EX, 8, rows), F32),
            pltpu.VMEM((EX, rows, LANE), BF16),
            pltpu.VMEM((2, 16, 2, RB, LANE), BF16),
            pltpu.VMEM((2, 16, 2, RB, LANE), BF16),
            pltpu.VMEM((2, 2, packed, LANE), BF16),
            pltpu.VMEM((2, EX, packed, LANE), BF16),
            pltpu.VMEM((2, 8, 2, packed, hidden), BF16),
            pltpu.VMEM((EX, hidden, 2 * LANE), BF16),
            pltpu.VMEM((EX, rows, LANE), F32),
            pltpu.VMEM((EX, rows, LANE), F32),
            pltpu.VMEM((2, 16, RB, 2 * LANE), BF16),
            pltpu.VMEM((2, 16, RB, 2 * LANE), BF16),
            pltpu.VMEM((2, rows, LANE), F32),
            pltpu.VMEM((rows, LANE), F32),
            pltpu.VMEM((packed, 16 * RB), BF16),
            pltpu.VMEM((16 * RB, packed), BF16),
            pltpu.VMEM((64 * RB, rows), BF16),
            pltpu.VMEM((32 * RB, rows), F32),
            pltpu.SemaphoreType.DMA((6,)),
        ]
        + sems(DP) + sems(EX) + sems(EX) + sems(EX) + sems(EX) + sems(2, 16)
        + sems(2, EX) + sems(EX) + sems(2, 8) + sems(2, 16) + sems(2) + sems(),
        compiler_params=pltpu.CompilerParams(
            collective_id=0, has_side_effects=True, vmem_limit_bytes=60 * 1024 * 1024
        ),
        name="layer",
    )(
        residual_in, attention_values, out_weight.T, norm_gain.reshape(EX, LANE),
        shared_gate, shared_up, shared_down, expert_gate, expert_up, expert_down,
        expert_ids.T, gate_weights.T,
    )


def solution(mesh):
    return jax.shard_map(
        shards,
        mesh=mesh,
        in_specs=(
            P("dp", "expert"),
            P("dp", "expert"),
            P("expert", "dp"),
            P(),
            P("expert", None),
            P("expert", None),
            P("expert", None),
            P("dp", "expert", None),
            P("dp", "expert", None),
            P("dp", "expert", None),
            P("dp", None),
            P("dp", None),
        ),
        out_specs=P("dp", "expert"),
        check_vma=False,
    )
```
